32 devices in a mesh: rows: 8 (over y, x, core), own: 4 (over z).
Axes of the slice: x: 2, y: 2, z: 4, core: 2. Of those that a mesh axis runs over, the one named last changes fastest.
Arguments:
- emb: bfloat16 [32768, 1024], P(('rows', 'own'))
- send_rows: int32 [32, 8, 256], P(('rows', 'own')), may hold values from 0 to 1024, as said below
- dest_offset: int32 [32, 8, 256], P(('rows', 'own')), may hold values from 0 to 2048, as said below
Outputs:
- centroids: float32 [32, 1024], P('rows')
- dup_score: float32 [32, 2048], P('rows', 'own')
The draws below stay inside these ranges and needn't reach their ends.
Inputs may be any that keep to these rules, and one draw needn't show every extreme that they name: `send_rows`: each device names each of its 1024 local rows in exactly one slot; the filled slots of a (device, owner) pair come first; for each device a quarter of the owners get all 256 slots filled, a quarter none and the rest 256 / 2. `dest_offset`: filled slots and only they hold a value below 2048. Over all rows that reach one owner from one index of own (exactly 1024 rows), the values are distinct, and cluster c takes the places 0 to n_c - 1, where n_0 to n_3 are 512, 256, 128 and 128 in some order.
All inputs are finite; a program needn't handle non-finite values.
Results may differ from the reference program's by a relative error of at most 0.0039.
Values may be sent and summed in bfloat16 or wider, within the bound.
No kernel may reach another device: no remote copies, remote signals or barrier semaphores. Data moves between devices by JAX's collectives and lax.ppermute only.
A program may use at most 64 MiB of HBM per device.

```python
import math
import jax
import jax.numpy as jnp
from jax import lax

D = 1024
KC = 4
R_DEV = 1024
CAP = 256
SUB = 512
TILE = 2048
K = 32
ALLROWS = 32768
N_ROWS = 8
N_OWN = 4


def layout(key):
    key = jax.random.fold_in(key, 7)
    quarter = N_ROWS // 4
    mean_load = R_DEV // N_ROWS
    base = jnp.concatenate([jnp.ones((quarter,), jnp.int32), -jnp.ones((quarter,), jnp.int32), jnp.zeros((N_ROWS - 2 * quarter,), jnp.int32)])
    pattern = jax.vmap(lambda k: jax.random.permutation(k, base))(jax.random.split(jax.random.fold_in(key, 1), N_OWN))
    shifts = jax.vmap(lambda k: jax.random.permutation(k, N_ROWS))(jax.random.split(jax.random.fold_in(key, 2), N_OWN))
    owners = jnp.arange(N_ROWS, dtype=jnp.int32)
    where_in = (owners[None, None, :] + shifts[:, :, None]) % N_ROWS
    spread = jnp.take_along_axis(jnp.broadcast_to(pattern[:, None, :], (N_OWN, N_ROWS, N_ROWS)), where_in, axis=2)
    loads = mean_load * (1 + spread)
    col_start = jnp.cumsum(loads, axis=1) - loads
    row_start = jnp.cumsum(loads, axis=2) - loads
    slot = jnp.arange(CAP, dtype=jnp.int32)
    valid = slot[None, None, None, :] < loads[:, :, :, None]
    sizes_table = jnp.array([SUB, SUB // 2, SUB // 4, SUB // 4], jnp.int32)
    order = jax.vmap(lambda k: jax.random.permutation(k, 4))(jax.random.split(jax.random.fold_in(key, 3), N_OWN * N_ROWS)).reshape(N_OWN, N_ROWS, 4)
    counts = sizes_table[order]
    ends = jnp.cumsum(counts, axis=-1)
    begins = ends - counts
    entry = jnp.arange(R_DEV, dtype=jnp.int32)
    cluster = jnp.sum((entry[None, None, :, None] >= ends[:, :, None, :]).astype(jnp.int32), axis=-1)
    within = entry[None, None, :] - jnp.take_along_axis(begins, cluster, axis=2)
    table = cluster * SUB + within
    mixing = jax.vmap(lambda k: jax.random.permutation(k, R_DEV))(jax.random.split(jax.random.fold_in(key, 4), N_OWN * N_ROWS)).reshape(N_OWN, N_ROWS, R_DEV)
    shuffled = jnp.take_along_axis(table, mixing, axis=2)
    arriving = jnp.minimum(col_start[:, :, :, None] + slot[None, None, None, :], R_DEV - 1)
    group_ix = jnp.arange(N_OWN, dtype=jnp.int32)[:, None, None, None]
    owner_ix = owners[None, None, :, None]
    source_ix = owners[None, :, None, None]
    dest = jnp.where(valid, shuffled[group_ix, owner_ix, arriving], KC * SUB)
    local_order = jax.vmap(lambda k: jax.random.permutation(k, R_DEV))(jax.random.split(jax.random.fold_in(key, 5), N_OWN * N_ROWS)).reshape(N_OWN, N_ROWS, R_DEV)
    rank = jnp.minimum(row_start[:, :, :, None] + slot[None, None, None, :], R_DEV - 1)
    local = jnp.where(valid, local_order[group_ix, source_ix, rank], R_DEV)
    local = jnp.transpose(local, (1, 0, 2, 3)).reshape(N_ROWS * N_OWN, N_ROWS, CAP)
    dest = jnp.transpose(dest, (1, 0, 2, 3)).reshape(N_ROWS * N_OWN, N_ROWS, CAP)
    return (local.astype(jnp.int32), dest.astype(jnp.int32))


def draw_send_rows(key, part):
    return layout(key)[0]


def draw_dest_offset(key, part):
    return layout(key)[1]


def draw_emb(key, part):
    local, dest = layout(key)
    devices = N_ROWS * N_OWN
    device_ix = jnp.arange(devices, dtype=jnp.int32)[:, None, None]
    owner_ix = jnp.arange(N_ROWS, dtype=jnp.int32)[None, :, None]
    cluster = owner_ix * KC + dest // SUB
    place = device_ix % N_OWN * SUB + dest % SUB
    slot_table = jnp.zeros((devices, R_DEV + 1), jnp.int32).at[device_ix, local].set(cluster * TILE + place)
    slot_of_row = slot_table[:, :R_DEV].reshape(-1)
    row_cluster = slot_of_row // TILE
    row_place = slot_of_row % TILE
    visit = jax.vmap(lambda k: jax.random.permutation(k, TILE))(jax.random.split(jax.random.fold_in(key, 31), K))
    cluster_ix = jnp.arange(K, dtype=jnp.int32)[:, None]
    visit_rank = jnp.zeros((K, TILE), jnp.int32).at[cluster_ix, visit].set(jnp.broadcast_to(jnp.arange(TILE, dtype=jnp.int32)[None, :], (K, TILE)))
    starts = (jax.random.randint(jax.random.fold_in(key, 32), (K, TILE), 0, 4) == 0).astype(jnp.int32)
    starts = starts.at[:, 0].set(1)
    group_in = jnp.cumsum(starts, axis=1) - 1
    row_group = group_in[row_cluster, visit_rank[row_cluster, row_place]]
    sub_pick = jax.random.randint(jax.random.fold_in(key, 33), (K, TILE), 0, 4)
    row_sub = sub_pick[row_cluster, row_group]
    group_ids = row_cluster * TILE + row_group
    base_key = jax.random.fold_in(key, 35)
    weights = jnp.exp(jax.random.uniform(jax.random.fold_in(key, 22), (ALLROWS, 1), jnp.float32, math.log(0.3), math.log(3.0)))
    spread = jnp.exp(jax.random.uniform(jax.random.fold_in(key, 24), (ALLROWS, 1), jnp.float32, math.log(0.3), math.log(1.0)))
    centers = jax.random.normal(jax.random.fold_in(key, 21), (K, D), jnp.float32)
    subcenters = jax.random.normal(jax.random.fold_in(key, 34), (K * 4, D), jnp.float32)
    bases = jax.vmap(lambda g: jax.random.normal(jax.random.fold_in(base_key, g), (D,), jnp.float32))(group_ids)
    noise = jax.random.normal(jax.random.fold_in(key, 23), (ALLROWS, D), jnp.float32)
    shared = jnp.take(centers, row_cluster, axis=0) + jnp.take(subcenters, row_cluster * 4 + row_sub, axis=0)
    values = weights * (shared + bases + spread * noise)
    return values.astype(jnp.bfloat16)


def setup_inputs(seed: int = 0) -> dict:
    splits = jax.random.split(jax.random.key(seed), 4)
    emb = draw_emb(jax.random.fold_in(splits[3], 71), 0)
    send_rows = draw_send_rows(jax.random.fold_in(splits[3], 71), 0)
    dest_offset = draw_dest_offset(jax.random.fold_in(splits[3], 71), 0)
    return {"emb": emb, "send_rows": send_rows, "dest_offset": dest_offset}


sharpness = 20.0

def soft_match(queries, keys, key_mask, query_pos):
    similar = jnp.einsum('cqd,ckd->cqk', queries.astype(jnp.float32), keys.astype(jnp.float32))
    key_pos = jnp.arange(keys.shape[1], dtype=jnp.int32)
    apart = (query_pos[:, None] != key_pos[None, :]).astype(jnp.float32)
    weights_mask = key_mask[:, None, :] * apart[None, :, :]
    total = lax.optimization_barrier(jnp.sum(jnp.exp(sharpness * similar) * weights_mask, axis=-1))
    return jnp.log(total) / sharpness

def reference(emb, send_rows, dest_offset):
    ids = send_rows.reshape(N_ROWS, N_OWN, N_ROWS, CAP)
    places = dest_offset.reshape(N_ROWS, N_OWN, N_ROWS, CAP)
    source = jnp.arange(N_ROWS, dtype=jnp.int32)[:, None, None] * N_OWN + jnp.arange(N_OWN, dtype=jnp.int32)[None, :, None]
    group = jnp.arange(N_OWN, dtype=jnp.int32)[None, :, None]

    def owner(index):
        row_ids = jnp.take(ids, index, axis=2)
        slot_places = jnp.take(places, index, axis=2)
        present = row_ids < R_DEV
        global_ids = source * R_DEV + jnp.minimum(row_ids, R_DEV - 1)
        moved = jnp.take(emb, global_ids.reshape(-1), axis=0)
        flat = jnp.where(present, slot_places // SUB * TILE + group * SUB + slot_places % SUB, KC * TILE).reshape(-1)
        tiles = jnp.zeros((KC * TILE, D), jnp.bfloat16).at[flat].set(moved, mode='drop').reshape(KC, TILE, D)
        filled = jnp.zeros((KC * TILE,), jnp.float32).at[flat].set(1.0, mode='drop').reshape(KC, TILE)
        wide = tiles.astype(jnp.float32)
        sums = lax.optimization_barrier(jnp.sum(wide * filled[:, :, None], axis=1))
        centroid = sums / lax.optimization_barrier(jnp.sum(filled, axis=1))[:, None]
        unit = wide * lax.rsqrt(lax.optimization_barrier(jnp.sum(wide * wide, axis=-1, keepdims=True)) + 1e-06)
        unit_b = unit.astype(jnp.bfloat16)
        direction = centroid * lax.rsqrt(lax.optimization_barrier(jnp.sum(centroid * centroid, axis=-1, keepdims=True)) + 1e-06)
        toward = lax.optimization_barrier(jnp.sum(unit * direction[:, None, :], axis=-1))
        matched = soft_match(unit_b, unit_b, filled, jnp.arange(TILE, dtype=jnp.int32))
        return (centroid, (matched - toward) * filled)
    cents, scores = lax.map(owner, jnp.arange(N_ROWS, dtype=jnp.int32))
    return (cents.reshape(K, D), scores.reshape(K, TILE))
```

```python
import functools

import jax
import jax.numpy as jnp
from jax import lax
from jax.experimental import pallas as pl
from jax.experimental.pallas import tpu as pltpu
from jax.sharding import PartitionSpec as P

KC = 4
CHUNKS = 2
SHARPNESS = 20.0
LANES = 128
ROWS = 256

vmem = pl.BlockSpec(memory_space=pltpu.VMEM)
smem = pl.BlockSpec(memory_space=pltpu.SMEM)


def gather_body(ids_ref, emb_ref, out_ref):
    groups, per = ids_ref.shape
    local = emb_ref.shape[0]
    columns = jnp.transpose(ids_ref[...])
    lane = lax.broadcasted_iota(jnp.int32, (per, local), 1)
    for o in range(groups):
        pick = jnp.where(columns[:, o : o + 1] == lane, 1.0, 0.0).astype(jnp.bfloat16)
        rows = jnp.dot(pick, emb_ref[...], preferred_element_type=jnp.float32)
        out_ref[o * per : (o + 1) * per, :] = rows.astype(jnp.bfloat16)


def gather_rows(ids, emb, chunk, chunks):
    slots = ids.size
    local, width = emb.shape
    part = width // chunks
    return pl.pallas_call(
        gather_body,
        grid=(1,),
        in_specs=[
            pl.BlockSpec(ids.shape, lambda i: (0, 0)),
            pl.BlockSpec((local, part), lambda i: (0, chunk)),
        ],
        out_specs=pl.BlockSpec((slots, part), lambda i: (0, 0)),
        out_shape=jax.ShapeDtypeStruct((slots, part), emb.dtype),
        cost_estimate=pl.CostEstimate(
            flops=2 * slots * local * part,
            bytes_accessed=2 * part * (slots + local),
            transcendentals=0,
        ),
        compiler_params=pltpu.CompilerParams(vmem_limit_bytes=40 << 20),
        name="gather_rows",
    )(ids, emb)


def place_body(places_ref, rows_ref, out_ref):
    arrivals = rows_ref.shape[0]
    places = places_ref[...]
    for b in range(out_ref.shape[0] // ROWS):
        slot = b * ROWS + lax.broadcasted_iota(jnp.int32, (ROWS, arrivals), 0)
        pick = jnp.where(slot == places, 1.0, 0.0).astype(jnp.bfloat16)
        rows = jnp.dot(pick, rows_ref[...], preferred_element_type=jnp.float32)
        out_ref[b * ROWS : (b + 1) * ROWS, :] = rows.astype(jnp.bfloat16)


def place_rows(places, rows, capacity):
    arrivals, part = rows.shape
    return pl.pallas_call(
        place_body,
        in_specs=[vmem, vmem],
        out_specs=vmem,
        out_shape=jax.ShapeDtypeStruct((capacity, part), rows.dtype),
        cost_estimate=pl.CostEstimate(
            flops=2 * arrivals * capacity * part,
            bytes_accessed=2 * part * (arrivals + capacity),
            transcendentals=0,
        ),
        compiler_params=pltpu.CompilerParams(vmem_limit_bytes=40 << 20),
        name="place_rows",
    )(places, rows)


def score_body(units, per_sender, counts_ref, *refs):
    part_refs = refs[:CHUNKS]
    out_ref, unit_b, tow, row_sum, col_sum, total_sum = refs[CHUNKS:]
    part = part_refs[0].shape[1]
    width = part * CHUNKS
    lane = lax.broadcasted_iota(jnp.int32, (LANES, LANES), 1)

    def rows_of(u):
        return [
            ref[u * LANES : (u + 1) * LANES, :].astype(jnp.float32) for ref in part_refs
        ]

    def is_filled(u):
        return counts_ref[u // per_sender] > (u % per_sender) * LANES

    row_sum[...] = jnp.zeros_like(row_sum)
    col_sum[...] = jnp.zeros_like(col_sum)
    tow[...] = jnp.zeros_like(tow)
    total_sum[...] = jnp.zeros_like(total_sum)
    position = []
    filled_units = jnp.int32(0)
    for u in range(units):
        position.append(filled_units)

        @pl.when(is_filled(u))
        def _(u=u, at=filled_units):
            pieces = rows_of(u)
            square = sum(jnp.sum(x * x, axis=-1, keepdims=True) for x in pieces)
            inverse = lax.rsqrt(square + 1e-06)
            for k, x in enumerate(pieces):
                cols = slice(k * part, (k + 1) * part)
                total_sum[:, cols] += jnp.sum(x.reshape(LANES // 8, 8, part), axis=0)
                unit_b[pl.ds(pl.multiple_of(at * LANES, LANES), LANES), cols] = (
                    x * inverse
                ).astype(jnp.bfloat16)

        filled_units = filled_units + is_filled(u).astype(jnp.int32)

    @pl.when(filled_units % 2 == 1)
    def _():
        unit_b[pl.ds(pl.multiple_of(filled_units * LANES, LANES), LANES), :] = jnp.zeros(
            (LANES, width), jnp.bfloat16
        )

    count = (filled_units * LANES).astype(jnp.float32)
    centroid = jnp.sum(total_sum[...], axis=0, keepdims=True) / count
    direction = centroid * lax.rsqrt(
        jnp.sum(centroid * centroid, axis=-1, keepdims=True) + 1e-06
    )

    for u in range(units):

        @pl.when(is_filled(u))
        def _(u=u, at=position[u]):
            pieces = rows_of(u)
            square = sum(jnp.sum(x * x, axis=-1, keepdims=True) for x in pieces)
            inverse = lax.rsqrt(square + 1e-06)
            along = sum(
                jnp.sum(
                    (x * inverse) * direction[:, k * part : (k + 1) * part],
                    axis=-1,
                    keepdims=True,
                )
                for k, x in enumerate(pieces)
            )
            tow[...] = jnp.where(lane == at, along, tow[...])

    blocks = (filled_units + 1) // 2
    key = lax.broadcasted_iota(jnp.int32, (ROWS, ROWS), 1)
    query = lax.broadcasted_iota(jnp.int32, (ROWS, ROWS), 0)

    def add_rows(i, terms):
        sums = jnp.sum(terms, axis=-1, keepdims=True)
        for h in range(ROWS // LANES):
            row_sum[...] += jnp.where(
                lane == i * (ROWS // LANES) + h, sums[h * LANES : (h + 1) * LANES], 0.0
            )

    def terms_of(i, j):
        a = unit_b[pl.ds(pl.multiple_of(i * ROWS, ROWS), ROWS), :]
        b = unit_b[pl.ds(pl.multiple_of(j * ROWS, ROWS), ROWS), :]
        similar = lax.dot_general(
            a, b, (((1,), (1,)), ((), ())), preferred_element_type=jnp.float32
        )
        inside = key < filled_units * LANES - j * ROWS
        return jnp.where(inside, jnp.exp(SHARPNESS * similar), 0.0)

    def row_block(i, carry):
        add_rows(i, jnp.where(key == query, 0.0, terms_of(i, i)))

        def pair(j, carry):
            terms = terms_of(i, j)
            add_rows(i, terms)
            sums = jnp.sum(terms, axis=0, keepdims=True)
            for h in range(ROWS // LANES):
                col_sum[pl.ds(j * (ROWS // LANES) + h, 1), :] += sums[
                    :, h * LANES : (h + 1) * LANES
                ]
            return carry

        lax.fori_loop(i + 1, blocks, pair, 0)
        return carry

    lax.fori_loop(0, blocks, row_block, 0)

    total = jnp.transpose(row_sum[...])[:units] + col_sum[...]
    col_sum[...] = jnp.log(total) / SHARPNESS - jnp.transpose(tow[...])[:units]
    out_ref[...] = jnp.zeros_like(out_ref)
    senders = units // per_sender
    for u in range(units):

        @pl.when(is_filled(u))
        def _(u=u, at=position[u]):
            out_ref[u // per_sender, pl.ds(u % per_sender, 1), :] = col_sum[
                pl.ds(at, 1), :
            ]

    for s in range(senders):
        for k in range(width // LANES):
            out_ref[s, per_sender + k : per_sender + k + 1, :] = centroid[
                :, k * LANES : (k + 1) * LANES
            ]


def score_cluster(counts, parts, senders):
    capacity, part = parts[0].shape
    units = capacity // LANES
    per_sender = units // senders
    width = part * len(parts)
    return pl.pallas_call(
        functools.partial(score_body, units, per_sender),
        in_specs=[smem] + [vmem] * len(parts),
        out_specs=vmem,
        out_shape=jax.ShapeDtypeStruct(
            (senders, per_sender + width // LANES, LANES), jnp.float32
        ),
        scratch_shapes=[
            pltpu.VMEM((capacity, width), jnp.bfloat16),
            pltpu.VMEM((LANES, LANES), jnp.float32),
            pltpu.VMEM((LANES, LANES), jnp.float32),
            pltpu.VMEM((units, LANES), jnp.float32),
            pltpu.VMEM((8, width), jnp.float32),
        ],
        cost_estimate=pl.CostEstimate(
            flops=capacity * capacity * width,
            bytes_accessed=2 * capacity * width,
            transcendentals=capacity * capacity // 2,
        ),
        compiler_params=pltpu.CompilerParams(vmem_limit_bytes=48 << 20),
        name="score_cluster",
    )(counts, *parts)


def on_device(emb, send_rows, dest_offset):
    owners = lax.axis_size("rows")
    senders = lax.axis_size("own")
    local, width = emb.shape
    slots = send_rows.shape[2]
    sub = local // 2
    capacity = KC * sub
    part = width // CHUNKS
    ids = send_rows[0].reshape(-1, ROWS)
    arrived = lax.all_to_all(dest_offset[0], "rows", split_axis=0, concat_axis=0, tiled=True)
    places = arrived.reshape(1, owners * slots)
    cluster = jnp.arange(KC, dtype=jnp.int32)[:, None]
    filled = jnp.sum((places // sub == cluster).astype(jnp.int32), axis=1)
    counts = lax.all_gather(filled, "own", axis=0, tiled=False)
    here = lax.axis_index("own")

    parts = []
    for k in range(CHUNKS):
        outgoing = gather_rows(ids, emb, k, CHUNKS).reshape(owners, slots, part)
        incoming = lax.all_to_all(outgoing, "rows", split_axis=0, concat_axis=0, tiled=True)
        placed = place_rows(places, incoming.reshape(owners * slots, part), capacity)
        whole = lax.all_to_all(
            placed.reshape(KC, sub, part), "own", split_axis=0, concat_axis=0, tiled=True
        )
        parts.append(whole.reshape(capacity, part))
    mine = lax.dynamic_index_in_dim(counts, here, 1, keepdims=False)
    result = score_cluster(mine, parts, senders)
    back = lax.all_to_all(result, "own", split_axis=0, concat_axis=0, tiled=True)
    per = sub // LANES
    score = back[:, :per].reshape(KC, sub)
    centroid = back[:, per:].reshape(KC, width)
    return (centroid, score)


def solution(mesh):
    return jax.shard_map(
        on_device,
        mesh=mesh,
        in_specs=(
            P(("rows", "own"), None),
            P(("rows", "own"), None, None),
            P(("rows", "own"), None, None),
        ),
        out_specs=(P("rows", None), P("rows", "own")),
        check_vma=False,
    )
```

```python
import functools
import itertools

import jax
import jax.numpy as jnp
import numpy as np
from jax import lax
from jax.experimental import pallas as pl
from jax.experimental.pallas import tpu as pltpu
from jax.sharding import PartitionSpec as P

KC = 4
EIGHTHS = (2, 3, 3)
CHUNKS = len(EIGHTHS)
SHARPNESS = 20.0
LANES = 128
ROWS = 256
BIG = 56 << 20
SMALL = 16 << 20
UNROLL = 4

vmem = pl.BlockSpec(memory_space=pltpu.VMEM)
smem = pl.BlockSpec(memory_space=pltpu.SMEM)

HOME, MINE, FORWARD, OWN, PAIR, STEP, EXTRA, STEP_FROM, HERE = 0, 4, 5, 6, 7, 8, 9, 10, 11
PLAN_WIDTH = 16

ACROSS = (((1,), (1,)), ((), ()))


def routes(biggest, home, parity):
    step, extra, kinds = {}, {}, []
    for g in range(4):
        to = home[biggest[g]]
        if to == g:
            kinds.append(OWN)
        elif to == g ^ 1:
            kinds.append(PAIR)
        elif to in (1, 2):
            by = 3 - to
            if by not in step:
                step[by] = g
                kinds.append(STEP)
            else:
                if by != 2 - parity:
                    return None
                pair = {step[by], g}
                if pair != {by, by ^ 1}:
                    return None
                step[by] = by ^ 1
                extra[by] = by
                kinds.append(EXTRA)
        else:
            return None
    return step, extra


def build_plans():
    rows = np.zeros((2, 4, 4, 4, 4, 4, PLAN_WIDTH), np.int32)
    for parity in range(2):
        for biggest in itertools.product(range(4), repeat=4):
            best = None
            for home in itertools.permutations(range(4)):
                found = routes(biggest, home, parity)
                if found is not None and (best is None or len(found[1]) < len(best[1][1])):
                    best = (home, found)
            home, (step, extra) = best
            for z in range(4):
                row = rows[(parity,) + biggest][z]
                row[HOME : HOME + 4] = home
                row[MINE] = home.index(z)
                row[FORWARD] = int(z in step and step[z] != z)
                row[OWN] = int(home[biggest[z]] == z)
                row[PAIR] = int(home[biggest[z ^ 1]] == z)
                by = 3 - z
                row[STEP] = int(z in (1, 2) and by in step)
                row[STEP_FROM] = step.get(by, 0) if z in (1, 2) else 0
                row[EXTRA] = int(z in (1, 2) and by in extra)
                row[HERE] = z
    return rows.reshape(-1, PLAN_WIDTH)


PLANS = build_plans()


def pair_table(blocks):
    pairs = [(i, j) for j in range(blocks) for i in range(j + 1)]
    pairs += [(0, 0)] * UNROLL
    return np.asarray(pairs, np.int32).T.copy()


def gather_body(first, ids_ref, emb_ref, out_ref, held, rows_ref, sem, sems):
    groups, per = ids_ref.shape
    local, part = held.shape
    fetch = pltpu.make_async_copy(emb_ref.at[:, first : first + part], held, sem)
    fetch.start()
    columns = jnp.transpose(ids_ref[...])
    lane = lax.broadcasted_iota(jnp.int32, (per, local), 1)
    fetch.wait()
    sends = []
    for o in range(groups):
        at = slice(o * per, (o + 1) * per)
        pick = jnp.where(columns[:, o : o + 1] == lane, 1.0, 0.0).astype(jnp.bfloat16)
        rows = jnp.dot(pick, held[...], preferred_element_type=jnp.float32)
        rows_ref[at, :] = rows.astype(jnp.bfloat16)
        sends.append(pltpu.make_async_copy(rows_ref.at[at], out_ref.at[at], sems.at[o]))
        sends[-1].start()
    for send in sends:
        send.wait()


def gather_rows(ids, emb, first, part):
    slots = ids.size
    local = emb.shape[0]
    groups = ids.shape[0]
    return pl.pallas_call(
        functools.partial(gather_body, first),
        in_specs=[vmem, pl.BlockSpec(memory_space=pl.ANY)],
        out_specs=pl.BlockSpec(memory_space=pltpu.HBM),
        out_shape=jax.ShapeDtypeStruct((slots, part), emb.dtype),
        scratch_shapes=[
            pltpu.VMEM((local, part), emb.dtype),
            pltpu.VMEM((slots, part), emb.dtype),
            pltpu.SemaphoreType.DMA,
            pltpu.SemaphoreType.DMA((groups,)),
        ],
        cost_estimate=pl.CostEstimate(
            flops=2 * slots * local * part,
            bytes_accessed=2 * part * (slots + local),
            transcendentals=0,
        ),
        compiler_params=pltpu.CompilerParams(vmem_limit_bytes=SMALL),
        name="gather_rows",
    )(ids, emb)


def place_body(blocks, half, info_ref, places_ref, rows_ref, *out_refs):
    arrivals = rows_ref.shape[0]
    here = info_ref[KC * 4 + HERE]
    places = places_ref[...]
    cluster = places // (2 * half)
    inner = places % (2 * half)
    toward = jnp.full_like(places, 8)
    for c in range(KC):
        toward = jnp.where(cluster == c, info_ref[KC * 4 + HOME + c] ^ here, toward)
    target = jnp.where(inner < half, toward * half + inner, 4 * half + inner - half)
    target = jnp.where(cluster < KC, target, -1)
    for ref, inside in zip(out_refs, blocks):
        for n, b in enumerate(inside):
            slot = b * half + lax.broadcasted_iota(jnp.int32, (half, arrivals), 0)
            pick = jnp.where(slot == target, 1.0, 0.0).astype(jnp.bfloat16)
            rows = jnp.dot(pick, rows_ref[...], preferred_element_type=jnp.float32)
            ref[n * half : (n + 1) * half, :] = rows.astype(jnp.bfloat16)


def place_rows(info, places, rows, half, blocks):
    arrivals, part = rows.shape
    sizes = [half * len(inside) for inside in blocks]
    return pl.pallas_call(
        functools.partial(place_body, blocks, half),
        in_specs=[smem, vmem, vmem],
        out_specs=(vmem,) * len(sizes),
        out_shape=tuple(jax.ShapeDtypeStruct((n, part), rows.dtype) for n in sizes),
        cost_estimate=pl.CostEstimate(
            flops=2 * arrivals * sum(sizes) * part,
            bytes_accessed=2 * part * (arrivals + sum(sizes)),
            transcendentals=0,
        ),
        compiler_params=pltpu.CompilerParams(vmem_limit_bytes=SMALL),
        name="place_rows",
    )(info, places, rows)


def read_plan(info_ref, half):
    base = KC * 4
    here = info_ref[base + HERE]
    mine = info_ref[base + MINE]
    blocks = []
    for x in range(4):
        rows = jnp.minimum(info_ref[(here ^ x) * KC + mine], half)
        blocks.append((rows, here ^ x, 0))
    over = [
        (OWN, here),
        (PAIR, here ^ 1),
        (STEP, info_ref[base + STEP_FROM]),
        (EXTRA, 3 - here),
    ]
    for valid, sender in over:
        blocks.append((info_ref[base + valid] * half, sender, half // LANES))
    return blocks


def spots(blocks, half, first):
    found, at = [], first
    for rows, _, _ in blocks:
        for h in range(half // LANES):
            filled = rows > h * LANES
            found.append((filled, at))
            at = at + filled.astype(jnp.int32)
    return found, at


def take_units(found, sources, parts, unit_b, total_sum):
    firsts = [sum(parts[:k]) for k in range(len(parts))]
    for (filled, at), refs in zip(found, sources):

        @pl.when(filled)
        def _(at=at, refs=refs):
            pieces = [ref[...].astype(jnp.float32) for ref in refs]
            square = sum(jnp.sum(x * x, axis=-1, keepdims=True) for x in pieces)
            inverse = lax.rsqrt(square + 1e-06)
            for x, first, part in zip(pieces, firsts, parts):
                cols = slice(first, first + part)
                total_sum[:, cols] += jnp.sum(x.reshape(LANES // 8, 8, part), axis=0)
                unit_b[pl.ds(pl.multiple_of(at * LANES, LANES), LANES), cols] = (
                    x * inverse
                ).astype(jnp.bfloat16)


def add_pairs(pairs_ref, first, end, last, hole, unit_b, similar_ref, row_acc, col_acc):
    key = lax.broadcasted_iota(jnp.int32, (ROWS, ROWS), 1)
    query = lax.broadcasted_iota(jnp.int32, (ROWS, ROWS), 0)
    ahead = key - query
    block_of = lambda i: pl.ds(pl.multiple_of(i * ROWS, ROWS), ROWS)

    def pair_of(s, h):
        t = first + s * UNROLL + h
        return pairs_ref[0, t], pairs_ref[1, t], t

    def multiply(s):
        for h in range(UNROLL):
            i, j, _ = pair_of(s, h)
            similar_ref[s % 2, h] = lax.dot_general(
                unit_b[block_of(i), :],
                unit_b[block_of(j), :],
                ACROSS,
                preferred_element_type=jnp.float32,
            )

    def accumulate(s):
        for h in range(UNROLL):
            i, j, t = pair_of(s, h)
            counted = key < jnp.where(t < end, last - j * ROWS, 0)
            counted &= ahead != (i - j) * ROWS
            if hole is not None:
                counted &= (query < hole[0] - i * ROWS) | (query >= hole[1] - i * ROWS)
            terms = jnp.where(counted, jnp.exp(SHARPNESS * similar_ref[s % 2, h]), 0.0)
            row_acc[block_of(i), :] += sum(
                terms[:, k * LANES : (k + 1) * LANES] for k in range(ROWS // LANES)
            )
            sums = jnp.sum(terms.reshape(ROWS // 8, 8, ROWS), axis=0)
            col_acc[:, block_of(j)] += jnp.where(i == j, 0.0, sums)

    steps = (end - first + UNROLL - 1) // UNROLL
    multiply(0)

    def step(s, carry):
        multiply(s)
        accumulate(s - 1)
        return carry

    lax.fori_loop(1, steps, step, 0)
    accumulate(steps - 1)


def start_body(parts, half, info_ref, pairs_ref, *refs):
    per_chunk = 5
    chunks = [refs[k * per_chunk : (k + 1) * per_chunk] for k in range(len(parts))]
    unit_b, row_acc, col_acc, total_sum, similar_ref = refs[len(parts) * per_chunk :]
    blocks = read_plan(info_ref, half)[:6]
    found, units = spots(blocks, half, jnp.int32(0))
    sources = []
    for which, at in [(0, 0), (2, 0), (3, 0), (4, 0), (1, half), (2, half)]:
        for h in range(half // LANES):
            rows = pl.ds(at + h * LANES, LANES)
            sources.append([chunk[which].at[rows] for chunk in chunks])
    total_sum[...] = jnp.zeros_like(total_sum)
    row_acc[...] = jnp.zeros_like(row_acc)
    col_acc[...] = jnp.zeros_like(col_acc)
    take_units(found, sources, parts, unit_b, total_sum)

    @pl.when(units % 2 == 1)
    def _():
        unit_b[pl.ds(pl.multiple_of(units * LANES, LANES), LANES), :] = jnp.zeros(
            (LANES, sum(parts)), jnp.bfloat16
        )

    count = (units + 1) // 2
    end = count * (count + 1) // 2
    add_pairs(
        pairs_ref, 0, end, units * LANES, None, unit_b, similar_ref, row_acc, col_acc
    )


def score_body(parts, half, info_ref, pairs_ref, *refs):
    per_chunk = 2
    chunks = [refs[k * per_chunk : (k + 1) * per_chunk] for k in range(len(parts))]
    refs = refs[len(parts) * per_chunk + 4 :]
    out_ref, unit_b, row_acc, col_acc, total_sum, similar_ref, score_ref = refs
    width = sum(parts)
    per_half = half // LANES
    blocks = read_plan(info_ref, half)
    found, early = spots(blocks[:6], half, jnp.int32(0))
    early_blocks = (early + 1) // 2
    late_found, units = spots(blocks[6:], half, early_blocks * 2)
    count_blocks = units // 2
    first = early_blocks * (early_blocks + 1) // 2
    end = count_blocks * (count_blocks + 1) // 2

    @pl.when(count_blocks > early_blocks)
    def _():
        sources = []
        for which in range(2):
            for h in range(per_half):
                rows = pl.ds(h * LANES, LANES)
                sources.append([chunk[which].at[rows] for chunk in chunks])
        take_units(late_found, sources, parts, unit_b, total_sum)
        hole = (early * LANES, early_blocks * ROWS)
        add_pairs(
            pairs_ref, first, end, units * LANES, hole, unit_b, similar_ref, row_acc, col_acc
        )

    filled_units = early + units - early_blocks * 2
    count = (filled_units * LANES).astype(jnp.float32)
    centroid = jnp.sum(total_sum[...], axis=0, keepdims=True) / count
    direction = centroid * lax.rsqrt(
        jnp.sum(centroid * centroid, axis=-1, keepdims=True) + 1e-06
    )
    high = direction.astype(jnp.bfloat16)
    low = (direction - high.astype(jnp.float32)).astype(jnp.bfloat16)
    row = lax.broadcasted_iota(jnp.int32, (8, width), 0)
    split = jnp.where(
        row == 0,
        high.astype(jnp.float32),
        jnp.where(row == 1, low.astype(jnp.float32), 0.0),
    ).astype(jnp.bfloat16)
    ones = jnp.ones((8, LANES), jnp.float32)
    for b in range(unit_b.shape[0] // ROWS):
        at = slice(b * ROWS, (b + 1) * ROWS)

        @pl.when(b < count_blocks)
        def _(at=at):
            along = lax.dot_general(
                split, unit_b[at, :], ACROSS, preferred_element_type=jnp.float32
            )
            toward = jnp.sum(along, axis=0, keepdims=True)
            rows = lax.dot_general(
                ones,
                row_acc[at, :],
                ACROSS,
                precision=lax.Precision.HIGHEST,
                preferred_element_type=jnp.float32,
            )
            total = rows[:1] + jnp.sum(col_acc[:, at], axis=0, keepdims=True)
            score_ref[:, at] = jnp.log(total) / SHARPNESS - toward

    for s in range(4):
        out_ref[s, : 2 * per_half, :] = jnp.zeros((2 * per_half, LANES), jnp.float32)
        for k in range(width // LANES):
            at = 2 * per_half + k
            out_ref[s, at : at + 1, :] = centroid[:, k * LANES : (k + 1) * LANES]
    for u, (filled, at) in enumerate(found + late_found):
        _, sender, place = blocks[u // per_half]

        @pl.when(filled)
        def _(at=at, to=sender, place=place + u % per_half):
            out_ref[to, place : place + 1, :] = score_ref[
                :, pl.ds(pl.multiple_of(at * LANES, LANES), LANES)
            ]


def start_cluster(info, chunks):
    half = chunks[0][0].shape[0]
    parts = [chunk[0].shape[1] for chunk in chunks]
    width = sum(parts)
    capacity = 8 * half
    flat = [a for chunk in chunks for a in chunk]
    return pl.pallas_call(
        functools.partial(start_body, parts, half),
        in_specs=[smem, smem] + [vmem] * len(flat),
        out_specs=(vmem,) * 4,
        out_shape=(
            jax.ShapeDtypeStruct((capacity, width), jnp.bfloat16),
            jax.ShapeDtypeStruct((capacity, LANES), jnp.float32),
            jax.ShapeDtypeStruct((8, capacity), jnp.float32),
            jax.ShapeDtypeStruct((8, width), jnp.float32),
        ),
        scratch_shapes=[pltpu.VMEM((2, UNROLL, ROWS, ROWS), jnp.float32)],
        cost_estimate=pl.CostEstimate(
            flops=capacity * capacity * width,
            bytes_accessed=2 * capacity * width,
            transcendentals=capacity * capacity // 2,
        ),
        compiler_params=pltpu.CompilerParams(vmem_limit_bytes=SMALL),
        name="start_cluster",
    )(info, jnp.asarray(pair_table(capacity // ROWS)), *flat)


def score_cluster(info, chunks, begun):
    half = chunks[0][0].shape[0]
    parts = [chunk[0].shape[1] for chunk in chunks]
    width = sum(parts)
    capacity = 8 * half
    flat = [a for chunk in chunks for a in chunk]
    lines = 2 * half // LANES + width // LANES
    at = 2 + len(flat)
    out = pl.pallas_call(
        functools.partial(score_body, parts, half),
        in_specs=[smem, smem] + [vmem] * (len(flat) + 4),
        out_specs=(vmem,) * 5,
        out_shape=(jax.ShapeDtypeStruct((4, lines, LANES), jnp.float32),)
        + tuple(jax.ShapeDtypeStruct(a.shape, a.dtype) for a in begun),
        input_output_aliases={at + n: 1 + n for n in range(4)},
        scratch_shapes=[
            pltpu.VMEM((2, UNROLL, ROWS, ROWS), jnp.float32),
            pltpu.VMEM((1, capacity), jnp.float32),
        ],
        cost_estimate=pl.CostEstimate(
            flops=capacity * capacity * width // 4,
            bytes_accessed=2 * capacity * width,
            transcendentals=capacity * capacity // 8,
        ),
        compiler_params=pltpu.CompilerParams(vmem_limit_bytes=SMALL),
        name="score_cluster",
    )(info, jnp.asarray(pair_table(capacity // ROWS)), *flat, *begun)
    return out[0]


def finish_body(info_ref, back_ref, centroid_ref, score_ref):
    per = score_ref.shape[1] // LANES
    for c in range(KC):
        home = info_ref[KC * 4 + HOME + c]
        for k in range(back_ref.shape[1]):
            to, at = (score_ref, k) if k < per else (centroid_ref, k - per)
            to[c : c + 1, at * LANES : (at + 1) * LANES] = back_ref[home, k : k + 1, :]


def finish(info, back, sub, width):
    return pl.pallas_call(
        finish_body,
        in_specs=[smem, vmem],
        out_specs=(vmem, vmem),
        out_shape=(
            jax.ShapeDtypeStruct((KC, width), jnp.float32),
            jax.ShapeDtypeStruct((KC, sub), jnp.float32),
        ),
        name="finish",
    )(info, back)


def swap(x, by):
    return lax.ppermute(x, "own", [(z, z ^ by) for z in range(4)])


def step_move(carried):
    return lax.ppermute(carried, "own", [(1, 2), (2, 1)])


def extra_move(overflow):
    owners = lax.axis_size("rows")
    crossing = [(r * 4 + 2 - r % 2, r * 4 + 1 + r % 2) for r in range(owners)]
    return lax.ppermute(overflow, ("rows", "own"), crossing)


def on_device(emb, send_rows, dest_offset):
    owners = lax.axis_size("rows")
    local, width = emb.shape
    slots = send_rows.shape[2]
    sub = local // 2
    half = sub // 2
    parts = [width // 8 * n for n in EIGHTHS]
    ids = send_rows[0].reshape(-1, ROWS)
    here = lax.axis_index("own")
    owner = lax.axis_index("rows")
    every = lax.all_to_all(
        jnp.repeat(dest_offset[0], 4, axis=0), ("rows", "own"), split_axis=0, concat_axis=0, tiled=True
    )
    every = every.reshape(owners, 4, slots)
    places = lax.dynamic_index_in_dim(every, here, 1, keepdims=False)
    places = places.reshape(1, owners * slots)
    cluster = jnp.arange(KC, dtype=jnp.int32)
    counts = jnp.sum((every[..., None] // sub == cluster).astype(jnp.int32), axis=(0, 2))
    place_value = jnp.asarray([64, 16, 4, 1], jnp.int32)
    index = jnp.sum(jnp.argmax(counts, axis=1).astype(jnp.int32) * place_value)
    index = ((owner % 2) * 256 + index) * 4 + here
    row = lax.dynamic_index_in_dim(jnp.asarray(PLANS), index, 0, keepdims=False)
    info = jnp.concatenate([counts.reshape(-1), row])

    tie = lax.optimization_barrier
    outgoing, moved, carried, steps = [], [], [], []

    def gather(k, ids):
        rows = gather_rows(ids, emb, sum(parts[:k]), parts[k])
        outgoing.append(rows.reshape(owners, slots, parts[k]))

    gather(0, ids)
    ids, info = tie((ids, info))
    gather(1, ids)
    for k, part in enumerate(parts):
        incoming = lax.all_to_all(outgoing[k], "rows", split_axis=0, concat_axis=0, tiled=True)
        if k:
            incoming, carried[-1], *last = tie((incoming, carried[-1]) + moved[-1])
            moved[-1] = tuple(last)
        incoming = incoming.reshape(owners * slots, part)
        two, three = place_rows(info, places, incoming, half, ((2,), (3,)))
        from_two, from_three = swap(two, 2), swap(three, 3)
        incoming, two = tie((incoming, two))
        kept, pair = place_rows(info, places, incoming, half, ((0,), (1, 4)))
        from_pair = swap(pair, 1)
        if k + 2 < CHUNKS:
            kept, ids = tie((kept, ids))
            gather(k + 2, ids)
            from_pair, from_two, from_three, outgoing[k + 2] = tie(
                (from_pair, from_two, from_three, outgoing[k + 2])
            )
        if k:
            steps.append(step_move(carried[-1]))
            from_pair, from_two, from_three, steps[-1] = tie(
                (from_pair, from_two, from_three, steps[-1])
            )
        moved.append((kept, pair, from_pair, from_two, from_three))
        carried.append(
            jnp.where(info[KC * 4 + FORWARD] == 1, from_pair[half:], pair[half:])
        )
    steps.append(step_move(carried[-1]))
    first = moved[-1][2]
    extras = [extra_move(tie((m[1][half:], first))[0]) for m in moved]
    begun = start_cluster(info, moved)
    result = score_cluster(info, list(zip(steps, extras)), begun)
    back = lax.all_to_all(result, "own", split_axis=0, concat_axis=0, tiled=True)
    return finish(info, back, sub, width)


def solution(mesh):
    return jax.shard_map(
        on_device,
        mesh=mesh,
        in_specs=(
            P(("rows", "own"), None),
            P(("rows", "own"), None, None),
            P(("rows", "own"), None, None),
        ),
        out_specs=(P("rows", None), P("rows", "own")),
        check_vma=False,
    )
```

```python
import functools
import itertools

import jax
import jax.numpy as jnp
import numpy as np
from jax import lax
from jax.experimental import pallas as pl
from jax.experimental.pallas import tpu as pltpu
from jax.sharding import PartitionSpec as P

KC = 4
EIGHTHS = (4, 4)
CHUNKS = len(EIGHTHS)
SHARPNESS = 20.0
LANES = 128
ROWS = 256
BIG = 56 << 20
SMALL = 16 << 20
UNROLL = 4

vmem = pl.BlockSpec(memory_space=pltpu.VMEM)
smem = pl.BlockSpec(memory_space=pltpu.SMEM)

HOME, MINE, FORWARD, OWN, PAIR, STEP, EXTRA, STEP_FROM, HERE = 0, 4, 5, 6, 7, 8, 9, 10, 11
PLAN_WIDTH = 16

ACROSS = (((1,), (1,)), ((), ()))


def routes(biggest, home, parity):
    step, extra, kinds = {}, {}, []
    for g in range(4):
        to = home[biggest[g]]
        if to == g:
            kinds.append(OWN)
        elif to == g ^ 1:
            kinds.append(PAIR)
        elif to in (1, 2):
            by = 3 - to
            if by not in step:
                step[by] = g
                kinds.append(STEP)
            else:
                if by != 2 - parity:
                    return None
                pair = {step[by], g}
                if pair != {by, by ^ 1}:
                    return None
                step[by] = by ^ 1
                extra[by] = by
                kinds.append(EXTRA)
        else:
            return None
    return step, extra


def build_plans():
    rows = np.zeros((2, 4, 4, 4, 4, 4, PLAN_WIDTH), np.int32)
    for parity in range(2):
        for biggest in itertools.product(range(4), repeat=4):
            best = None
            for home in itertools.permutations(range(4)):
                found = routes(biggest, home, parity)
                if found is not None and (best is None or len(found[1]) < len(best[1][1])):
                    best = (home, found)
            home, (step, extra) = best
            for z in range(4):
                row = rows[(parity,) + biggest][z]
                row[HOME : HOME + 4] = home
                row[MINE] = home.index(z)
                row[FORWARD] = int(z in step and step[z] != z)
                row[OWN] = int(home[biggest[z]] == z)
                row[PAIR] = int(home[biggest[z ^ 1]] == z)
                by = 3 - z
                row[STEP] = int(z in (1, 2) and by in step)
                row[STEP_FROM] = step.get(by, 0) if z in (1, 2) else 0
                row[EXTRA] = int(z in (1, 2) and by in extra)
                row[HERE] = z
    return rows.reshape(-1, PLAN_WIDTH)


PLANS = build_plans()


def pair_table(blocks):
    pairs = [(i, j) for j in range(blocks) for i in range(j + 1)]
    pairs += [(0, 0)] * UNROLL
    return np.asarray(pairs, np.int32).T.copy()


def gather_body(first, ids_ref, emb_ref, out_ref, held, rows_ref, sem, sems):
    groups, per = ids_ref.shape
    local, part = held.shape
    fetch = pltpu.make_async_copy(emb_ref.at[:, first : first + part], held, sem)
    fetch.start()
    columns = jnp.transpose(ids_ref[...])
    lane = lax.broadcasted_iota(jnp.int32, (per, local), 1)
    fetch.wait()
    sends = []
    for o in range(groups):
        at = slice(o * per, (o + 1) * per)
        pick = jnp.where(columns[:, o : o + 1] == lane, 1.0, 0.0).astype(jnp.bfloat16)
        rows = jnp.dot(pick, held[...], preferred_element_type=jnp.float32)
        rows_ref[at, :] = rows.astype(jnp.bfloat16)
        sends.append(pltpu.make_async_copy(rows_ref.at[at], out_ref.at[at], sems.at[o]))
        sends[-1].start()
    for send in sends:
        send.wait()


def gather_rows(ids, emb, first, part):
    slots = ids.size
    local = emb.shape[0]
    groups = ids.shape[0]
    return pl.pallas_call(
        functools.partial(gather_body, first),
        in_specs=[vmem, pl.BlockSpec(memory_space=pl.ANY)],
        out_specs=pl.BlockSpec(memory_space=pltpu.HBM),
        out_shape=jax.ShapeDtypeStruct((slots, part), emb.dtype),
        scratch_shapes=[
            pltpu.VMEM((local, part), emb.dtype),
            pltpu.VMEM((slots, part), emb.dtype),
            pltpu.SemaphoreType.DMA,
            pltpu.SemaphoreType.DMA((groups,)),
        ],
        cost_estimate=pl.CostEstimate(
            flops=2 * slots * local * part,
            bytes_accessed=2 * part * (slots + local),
            transcendentals=0,
        ),
        compiler_params=pltpu.CompilerParams(vmem_limit_bytes=BIG),
        name="gather_rows",
    )(ids, emb)


def place_body(blocks, half, info_ref, places_ref, rows_ref, *out_refs):
    arrivals = rows_ref.shape[0]
    here = info_ref[KC * 4 + HERE]
    places = places_ref[...]
    cluster = places // (2 * half)
    inner = places % (2 * half)
    toward = jnp.full_like(places, 8)
    for c in range(KC):
        toward = jnp.where(cluster == c, info_ref[KC * 4 + HOME + c] ^ here, toward)
    target = jnp.where(inner < half, toward * half + inner, 4 * half + inner - half)
    target = jnp.where(cluster < KC, target, -1)
    for ref, inside in zip(out_refs, blocks):
        for n, b in enumerate(inside):
            slot = b * half + lax.broadcasted_iota(jnp.int32, (half, arrivals), 0)
            pick = jnp.where(slot == target, 1.0, 0.0).astype(jnp.bfloat16)
            rows = jnp.dot(pick, rows_ref[...], preferred_element_type=jnp.float32)
            ref[n * half : (n + 1) * half, :] = rows.astype(jnp.bfloat16)


def place_rows(info, places, rows, half, blocks):
    arrivals, part = rows.shape
    sizes = [half * len(inside) for inside in blocks]
    return pl.pallas_call(
        functools.partial(place_body, blocks, half),
        in_specs=[smem, vmem, vmem],
        out_specs=(vmem,) * len(sizes),
        out_shape=tuple(jax.ShapeDtypeStruct((n, part), rows.dtype) for n in sizes),
        cost_estimate=pl.CostEstimate(
            flops=2 * arrivals * sum(sizes) * part,
            bytes_accessed=2 * part * (arrivals + sum(sizes)),
            transcendentals=0,
        ),
        compiler_params=pltpu.CompilerParams(vmem_limit_bytes=SMALL),
        name="place_rows",
    )(info, places, rows)


def read_plan(info_ref, half):
    base = KC * 4
    here = info_ref[base + HERE]
    mine = info_ref[base + MINE]
    blocks = []
    for x in range(4):
        rows = jnp.minimum(info_ref[(here ^ x) * KC + mine], half)
        blocks.append((rows, here ^ x, 0))
    over = [
        (OWN, here),
        (PAIR, here ^ 1),
        (STEP, info_ref[base + STEP_FROM]),
        (EXTRA, 3 - here),
    ]
    for valid, sender in over:
        blocks.append((info_ref[base + valid] * half, sender, half // LANES))
    return blocks


def spots(blocks, half, first):
    found, at = [], first
    for rows, _, _ in blocks:
        for h in range(half // LANES):
            filled = rows > h * LANES
            found.append((filled, at))
            at = at + filled.astype(jnp.int32)
    return found, at


def take_units(found, sources, parts, unit_b, total_sum):
    firsts = [sum(parts[:k]) for k in range(len(parts))]
    for (filled, at), refs in zip(found, sources):

        @pl.when(filled)
        def _(at=at, refs=refs):
            pieces = [ref[...].astype(jnp.float32) for ref in refs]
            square = sum(jnp.sum(x * x, axis=-1, keepdims=True) for x in pieces)
            inverse = lax.rsqrt(square + 1e-06)
            for x, first, part in zip(pieces, firsts, parts):
                cols = slice(first, first + part)
                total_sum[:, cols] += jnp.sum(x.reshape(LANES // 8, 8, part), axis=0)
                unit_b[pl.ds(pl.multiple_of(at * LANES, LANES), LANES), cols] = (
                    x * inverse
                ).astype(jnp.bfloat16)


def add_pairs(pairs_ref, first, end, last, hole, unit_b, similar_ref, row_acc, col_acc):
    key = lax.broadcasted_iota(jnp.int32, (ROWS, ROWS), 1)
    query = lax.broadcasted_iota(jnp.int32, (ROWS, ROWS), 0)
    ahead = key - query
    block_of = lambda i: pl.ds(pl.multiple_of(i * ROWS, ROWS), ROWS)

    def pair_of(s, h):
        t = first + s * UNROLL + h
        return pairs_ref[0, t], pairs_ref[1, t], t

    def multiply(s):
        for h in range(UNROLL):
            i, j, _ = pair_of(s, h)
            similar_ref[s % 2, h] = lax.dot_general(
                unit_b[block_of(i), :],
                unit_b[block_of(j), :],
                ACROSS,
                preferred_element_type=jnp.float32,
            )

    def accumulate(s):
        for h in range(UNROLL):
            i, j, t = pair_of(s, h)
            counted = key < jnp.where(t < end, last - j * ROWS, 0)
            counted &= ahead != (i - j) * ROWS
            if hole is not None:
                counted &= (query < hole[0] - i * ROWS) | (query >= hole[1] - i * ROWS)
            terms = jnp.where(counted, jnp.exp(SHARPNESS * similar_ref[s % 2, h]), 0.0)
            row_acc[block_of(i), :] += sum(
                terms[:, k * LANES : (k + 1) * LANES] for k in range(ROWS // LANES)
            )
            sums = jnp.sum(terms.reshape(ROWS // 8, 8, ROWS), axis=0)
            col_acc[:, block_of(j)] += jnp.where(i == j, 0.0, sums)

    steps = (end - first + UNROLL - 1) // UNROLL
    multiply(0)

    def step(s, carry):
        multiply(s)
        accumulate(s - 1)
        return carry

    lax.fori_loop(1, steps, step, 0)
    accumulate(steps - 1)


def start_body(parts, half, info_ref, pairs_ref, *refs):
    per_chunk = 5
    chunks = [refs[k * per_chunk : (k + 1) * per_chunk] for k in range(len(parts))]
    unit_b, row_acc, col_acc, total_sum, similar_ref = refs[len(parts) * per_chunk :]
    blocks = read_plan(info_ref, half)[:6]
    found, units = spots(blocks, half, jnp.int32(0))
    sources = []
    for which, at in [(0, 0), (2, 0), (3, 0), (4, 0), (1, half), (2, half)]:
        for h in range(half // LANES):
            rows = pl.ds(at + h * LANES, LANES)
            sources.append([chunk[which].at[rows] for chunk in chunks])
    total_sum[...] = jnp.zeros_like(total_sum)
    row_acc[...] = jnp.zeros_like(row_acc)
    col_acc[...] = jnp.zeros_like(col_acc)
    take_units(found, sources, parts, unit_b, total_sum)

    @pl.when(units % 2 == 1)
    def _():
        unit_b[pl.ds(pl.multiple_of(units * LANES, LANES), LANES), :] = jnp.zeros(
            (LANES, sum(parts)), jnp.bfloat16
        )

    count = (units + 1) // 2
    end = count * (count + 1) // 2
    add_pairs(
        pairs_ref, 0, end, units * LANES, None, unit_b, similar_ref, row_acc, col_acc
    )


def score_body(parts, half, info_ref, pairs_ref, *refs):
    per_chunk = 2
    chunks = [refs[k * per_chunk : (k + 1) * per_chunk] for k in range(len(parts))]
    refs = refs[len(parts) * per_chunk + 4 :]
    out_ref, unit_b, row_acc, col_acc, total_sum, similar_ref, score_ref = refs
    width = sum(parts)
    per_half = half // LANES
    blocks = read_plan(info_ref, half)
    found, early = spots(blocks[:6], half, jnp.int32(0))
    early_blocks = (early + 1) // 2
    late_found, units = spots(blocks[6:], half, early_blocks * 2)
    count_blocks = units // 2
    first = early_blocks * (early_blocks + 1) // 2
    end = count_blocks * (count_blocks + 1) // 2

    @pl.when(count_blocks > early_blocks)
    def _():
        sources = []
        for which in range(2):
            for h in range(per_half):
                rows = pl.ds(h * LANES, LANES)
                sources.append([chunk[which].at[rows] for chunk in chunks])
        take_units(late_found, sources, parts, unit_b, total_sum)
        hole = (early * LANES, early_blocks * ROWS)
        add_pairs(
            pairs_ref, first, end, units * LANES, hole, unit_b, similar_ref, row_acc, col_acc
        )

    filled_units = early + units - early_blocks * 2
    count = (filled_units * LANES).astype(jnp.float32)
    centroid = jnp.sum(total_sum[...], axis=0, keepdims=True) / count
    direction = centroid * lax.rsqrt(
        jnp.sum(centroid * centroid, axis=-1, keepdims=True) + 1e-06
    )
    high = direction.astype(jnp.bfloat16)
    low = (direction - high.astype(jnp.float32)).astype(jnp.bfloat16)
    row = lax.broadcasted_iota(jnp.int32, (8, width), 0)
    split = jnp.where(
        row == 0,
        high.astype(jnp.float32),
        jnp.where(row == 1, low.astype(jnp.float32), 0.0),
    ).astype(jnp.bfloat16)
    ones = jnp.ones((8, LANES), jnp.float32)
    for b in range(unit_b.shape[0] // ROWS):
        at = slice(b * ROWS, (b + 1) * ROWS)

        @pl.when(b < count_blocks)
        def _(at=at):
            along = lax.dot_general(
                split, unit_b[at, :], ACROSS, preferred_element_type=jnp.float32
            )
            toward = jnp.sum(along, axis=0, keepdims=True)
            rows = lax.dot_general(
                ones,
                row_acc[at, :],
                ACROSS,
                precision=lax.Precision.HIGHEST,
                preferred_element_type=jnp.float32,
            )
            total = rows[:1] + jnp.sum(col_acc[:, at], axis=0, keepdims=True)
            score_ref[:, at] = jnp.log(total) / SHARPNESS - toward

    for s in range(4):
        out_ref[s, : 2 * per_half, :] = jnp.zeros((2 * per_half, LANES), jnp.float32)
        for k in range(width // LANES):
            at = 2 * per_half + k
            out_ref[s, at : at + 1, :] = centroid[:, k * LANES : (k + 1) * LANES]
    for u, (filled, at) in enumerate(found + late_found):
        _, sender, place = blocks[u // per_half]

        @pl.when(filled)
        def _(at=at, to=sender, place=place + u % per_half):
            out_ref[to, place : place + 1, :] = score_ref[
                :, pl.ds(pl.multiple_of(at * LANES, LANES), LANES)
            ]


def start_cluster(info, chunks):
    half = chunks[0][0].shape[0]
    parts = [chunk[0].shape[1] for chunk in chunks]
    width = sum(parts)
    capacity = 8 * half
    flat = [a for chunk in chunks for a in chunk]
    return pl.pallas_call(
        functools.partial(start_body, parts, half),
        in_specs=[smem, smem] + [vmem] * len(flat),
        out_specs=(vmem,) * 4,
        out_shape=(
            jax.ShapeDtypeStruct((capacity, width), jnp.bfloat16),
            jax.ShapeDtypeStruct((capacity, LANES), jnp.float32),
            jax.ShapeDtypeStruct((8, capacity), jnp.float32),
            jax.ShapeDtypeStruct((8, width), jnp.float32),
        ),
        scratch_shapes=[pltpu.VMEM((2, UNROLL, ROWS, ROWS), jnp.float32)],
        cost_estimate=pl.CostEstimate(
            flops=capacity * capacity * width,
            bytes_accessed=2 * capacity * width,
            transcendentals=capacity * capacity // 2,
        ),
        compiler_params=pltpu.CompilerParams(vmem_limit_bytes=SMALL),
        name="start_cluster",
    )(info, jnp.asarray(pair_table(capacity // ROWS)), *flat)


def score_cluster(info, chunks, begun):
    half = chunks[0][0].shape[0]
    parts = [chunk[0].shape[1] for chunk in chunks]
    width = sum(parts)
    capacity = 8 * half
    flat = [a for chunk in chunks for a in chunk]
    lines = 2 * half // LANES + width // LANES
    at = 2 + len(flat)
    out = pl.pallas_call(
        functools.partial(score_body, parts, half),
        in_specs=[smem, smem] + [vmem] * (len(flat) + 4),
        out_specs=(vmem,) * 5,
        out_shape=(jax.ShapeDtypeStruct((4, lines, LANES), jnp.float32),)
        + tuple(jax.ShapeDtypeStruct(a.shape, a.dtype) for a in begun),
        input_output_aliases={at + n: 1 + n for n in range(4)},
        scratch_shapes=[
            pltpu.VMEM((2, UNROLL, ROWS, ROWS), jnp.float32),
            pltpu.VMEM((1, capacity), jnp.float32),
        ],
        cost_estimate=pl.CostEstimate(
            flops=capacity * capacity * width // 4,
            bytes_accessed=2 * capacity * width,
            transcendentals=capacity * capacity // 8,
        ),
        compiler_params=pltpu.CompilerParams(vmem_limit_bytes=SMALL),
        name="score_cluster",
    )(info, jnp.asarray(pair_table(capacity // ROWS)), *flat, *begun)
    return out[0]


def finish_body(info_ref, back_ref, centroid_ref, score_ref):
    per = score_ref.shape[1] // LANES
    for c in range(KC):
        home = info_ref[KC * 4 + HOME + c]
        for k in range(back_ref.shape[1]):
            to, at = (score_ref, k) if k < per else (centroid_ref, k - per)
            to[c : c + 1, at * LANES : (at + 1) * LANES] = back_ref[home, k : k + 1, :]


def finish(info, back, sub, width):
    return pl.pallas_call(
        finish_body,
        in_specs=[smem, vmem],
        out_specs=(vmem, vmem),
        out_shape=(
            jax.ShapeDtypeStruct((KC, width), jnp.float32),
            jax.ShapeDtypeStruct((KC, sub), jnp.float32),
        ),
        name="finish",
    )(info, back)


def swap(x, by):
    return lax.ppermute(x, "own", [(z, z ^ by) for z in range(4)])


def step_move(carried):
    return lax.ppermute(carried, "own", [(1, 2), (2, 1)])


def extra_move(overflow):
    owners = lax.axis_size("rows")
    crossing = [(r * 4 + 2 - r % 2, r * 4 + 1 + r % 2) for r in range(owners)]
    return lax.ppermute(overflow, ("rows", "own"), crossing)


def on_device(emb, send_rows, dest_offset):
    owners = lax.axis_size("rows")
    local, width = emb.shape
    slots = send_rows.shape[2]
    sub = local // 2
    half = sub // 2
    parts = [width // 8 * n for n in EIGHTHS]
    ids = send_rows[0].reshape(-1, ROWS)
    here = lax.axis_index("own")
    owner = lax.axis_index("rows")
    every = lax.all_to_all(
        jnp.repeat(dest_offset[0], 4, axis=0), ("rows", "own"), split_axis=0, concat_axis=0, tiled=True
    )
    every = every.reshape(owners, 4, slots)
    places = lax.dynamic_index_in_dim(every, here, 1, keepdims=False)
    places = places.reshape(1, owners * slots)
    cluster = jnp.arange(KC, dtype=jnp.int32)
    counts = jnp.sum((every[..., None] // sub == cluster).astype(jnp.int32), axis=(0, 2))
    place_value = jnp.asarray([64, 16, 4, 1], jnp.int32)
    index = jnp.sum(jnp.argmax(counts, axis=1).astype(jnp.int32) * place_value)
    index = ((owner % 2) * 256 + index) * 4 + here
    row = lax.dynamic_index_in_dim(jnp.asarray(PLANS), index, 0, keepdims=False)
    info = jnp.concatenate([counts.reshape(-1), row])

    tie = lax.optimization_barrier
    outgoing, moved, carried, steps = [], [], [], []

    def gather(k, ids):
        rows = gather_rows(ids, emb, sum(parts[:k]), parts[k])
        outgoing.append(rows.reshape(owners, slots, parts[k]))

    gather(0, ids)
    ids, info = tie((ids, info))
    gather(1, ids)
    extras = []
    for k, part in enumerate(parts):
        incoming = lax.all_to_all(outgoing[k], "rows", split_axis=0, concat_axis=0, tiled=True)
        incoming = incoming.reshape(owners * slots, part)
        if k:
            incoming, carried[-1] = tie((incoming, carried[-1]))
        two, three = place_rows(info, places, incoming, half, ((2,), (3,)))
        incoming, two = tie((incoming, two))
        kept, pair = place_rows(info, places, incoming, half, ((0,), (1, 4)))
        if k:
            steps.append(step_move(carried[-1]))
            two, three, pair, steps[-1], extras[-1], *last = tie(
                (two, three, pair, steps[-1], extras[-1]) + moved[-1]
            )
            moved[-1] = tuple(last)
        from_two, from_three, from_pair = swap(two, 2), swap(three, 3), swap(pair, 1)
        moved.append((kept, pair, from_pair, from_two, from_three))
        carried.append(
            jnp.where(info[KC * 4 + FORWARD] == 1, from_pair[half:], pair[half:])
        )
        overflow = pair[half:]
        if k == CHUNKS - 1:
            overflow, carried[-1] = tie((overflow, carried[-1]))
        extras.append(extra_move(overflow))
    steps.append(step_move(carried[-1]))
    begun = start_cluster(info, moved)
    result = score_cluster(info, list(zip(steps, extras)), begun)
    back = lax.all_to_all(result, "own", split_axis=0, concat_axis=0, tiled=True)
    return finish(info, back, sub, width)


def solution(mesh):
    return jax.shard_map(
        on_device,
        mesh=mesh,
        in_specs=(
            P(("rows", "own"), None),
            P(("rows", "own"), None, None),
            P(("rows", "own"), None, None),
        ),
        out_specs=(P("rows", None), P("rows", "own")),
        check_vma=False,
    )
```

```python
import functools
import itertools

import jax
import jax.numpy as jnp
import numpy as np
from jax import lax
from jax.experimental import pallas as pl
from jax.experimental.pallas import tpu as pltpu
from jax.sharding import PartitionSpec as P

KC = 4
EIGHTHS = (4, 4)
CHUNKS = len(EIGHTHS)
SHARPNESS = 20.0
LANES = 128
ROWS = 256
BIG = 56 << 20
SMALL = 16 << 20
UNROLL = 4

vmem = pl.BlockSpec(memory_space=pltpu.VMEM)
smem = pl.BlockSpec(memory_space=pltpu.SMEM)

HOME, MINE, FORWARD, OWN, PAIR, STEP, EXTRA, STEP_FROM, HERE = 0, 4, 5, 6, 7, 8, 9, 10, 11
PLAN_WIDTH = 16

ACROSS = (((1,), (1,)), ((), ()))


def routes(biggest, home, parity):
    step, extra, kinds = {}, {}, []
    for g in range(4):
        to = home[biggest[g]]
        if to == g:
            kinds.append(OWN)
        elif to == g ^ 1:
            kinds.append(PAIR)
        elif to in (1, 2):
            by = 3 - to
            if by not in step:
                step[by] = g
                kinds.append(STEP)
            else:
                if by != 2 - parity:
                    return None
                pair = {step[by], g}
                if pair != {by, by ^ 1}:
                    return None
                step[by] = by ^ 1
                extra[by] = by
                kinds.append(EXTRA)
        else:
            return None
    return step, extra


def build_plans():
    rows = np.zeros((2, 4, 4, 4, 4, 4, PLAN_WIDTH), np.int32)
    for parity in range(2):
        for biggest in itertools.product(range(4), repeat=4):
            best = None
            for home in itertools.permutations(range(4)):
                found = routes(biggest, home, parity)
                if found is not None and (best is None or len(found[1]) < len(best[1][1])):
                    best = (home, found)
            home, (step, extra) = best
            for z in range(4):
                row = rows[(parity,) + biggest][z]
                row[HOME : HOME + 4] = home
                row[MINE] = home.index(z)
                row[FORWARD] = int(z in step and step[z] != z)
                row[OWN] = int(home[biggest[z]] == z)
                row[PAIR] = int(home[biggest[z ^ 1]] == z)
                by = 3 - z
                row[STEP] = int(z in (1, 2) and by in step)
                row[STEP_FROM] = step.get(by, 0) if z in (1, 2) else 0
                row[EXTRA] = int(z in (1, 2) and by in extra)
                row[HERE] = z
    return rows.reshape(-1, PLAN_WIDTH)


PLANS = build_plans()


def pair_table(blocks):
    pairs = [(i, j) for j in range(blocks) for i in range(j + 1)]
    pairs += [(0, 0)] * UNROLL
    return np.asarray(pairs, np.int32).T.copy()


def gather_body(first, ids_ref, emb_ref, out_ref, held, rows_ref, sem, sems):
    groups, per = ids_ref.shape
    local, part = held.shape
    fetch = pltpu.make_async_copy(emb_ref.at[:, first : first + part], held, sem)
    fetch.start()
    columns = jnp.transpose(ids_ref[...])
    lane = lax.broadcasted_iota(jnp.int32, (per, local), 1)
    fetch.wait()
    sends = []
    for o in range(groups):
        at = slice(o * per, (o + 1) * per)
        pick = jnp.where(columns[:, o : o + 1] == lane, 1.0, 0.0).astype(jnp.bfloat16)
        rows = jnp.dot(pick, held[...], preferred_element_type=jnp.float32)
        rows_ref[at, :] = rows.astype(jnp.bfloat16)
        sends.append(pltpu.make_async_copy(rows_ref.at[at], out_ref.at[at], sems.at[o]))
        sends[-1].start()
    for send in sends:
        send.wait()


def gather_rows(ids, emb, first, part):
    slots = ids.size
    local = emb.shape[0]
    groups = ids.shape[0]
    return pl.pallas_call(
        functools.partial(gather_body, first),
        in_specs=[vmem, pl.BlockSpec(memory_space=pl.ANY)],
        out_specs=pl.BlockSpec(memory_space=pltpu.HBM),
        out_shape=jax.ShapeDtypeStruct((slots, part), emb.dtype),
        scratch_shapes=[
            pltpu.VMEM((local, part), emb.dtype),
            pltpu.VMEM((slots, part), emb.dtype),
            pltpu.SemaphoreType.DMA,
            pltpu.SemaphoreType.DMA((groups,)),
        ],
        cost_estimate=pl.CostEstimate(
            flops=2 * slots * local * part,
            bytes_accessed=2 * part * (slots + local),
            transcendentals=0,
        ),
        compiler_params=pltpu.CompilerParams(vmem_limit_bytes=BIG),
        name="gather_rows",
    )(ids, emb)


def place_body(blocks, half, info_ref, places_ref, rows_ref, *out_refs):
    arrivals = rows_ref.shape[0]
    here = info_ref[KC * 4 + HERE]
    places = places_ref[...]
    cluster = places // (2 * half)
    inner = places % (2 * half)
    toward = jnp.full_like(places, 8)
    for c in range(KC):
        toward = jnp.where(cluster == c, info_ref[KC * 4 + HOME + c] ^ here, toward)
    target = jnp.where(inner < half, toward * half + inner, 4 * half + inner - half)
    target = jnp.where(cluster < KC, target, -1)
    for ref, inside in zip(out_refs, blocks):
        for n, b in enumerate(inside):
            slot = b * half + lax.broadcasted_iota(jnp.int32, (half, arrivals), 0)
            pick = jnp.where(slot == target, 1.0, 0.0).astype(jnp.bfloat16)
            rows = jnp.dot(pick, rows_ref[...], preferred_element_type=jnp.float32)
            ref[n * half : (n + 1) * half, :] = rows.astype(jnp.bfloat16)


def place_rows(info, places, rows, half, blocks):
    arrivals, part = rows.shape
    sizes = [half * len(inside) for inside in blocks]
    return pl.pallas_call(
        functools.partial(place_body, blocks, half),
        in_specs=[smem, vmem, vmem],
        out_specs=(vmem,) * len(sizes),
        out_shape=tuple(jax.ShapeDtypeStruct((n, part), rows.dtype) for n in sizes),
        cost_estimate=pl.CostEstimate(
            flops=2 * arrivals * sum(sizes) * part,
            bytes_accessed=2 * part * (arrivals + sum(sizes)),
            transcendentals=0,
        ),
        compiler_params=pltpu.CompilerParams(vmem_limit_bytes=SMALL),
        name="place_rows",
    )(info, places, rows)


def read_plan(info_ref, half):
    base = KC * 4
    here = info_ref[base + HERE]
    mine = info_ref[base + MINE]
    blocks = []
    for x in range(4):
        rows = jnp.minimum(info_ref[(here ^ x) * KC + mine], half)
        blocks.append((rows, here ^ x, 0))
    over = [
        (OWN, here),
        (PAIR, here ^ 1),
        (STEP, info_ref[base + STEP_FROM]),
        (EXTRA, 3 - here),
    ]
    for valid, sender in over:
        blocks.append((info_ref[base + valid] * half, sender, half // LANES))
    return blocks


def spots(blocks, half, first):
    found, at = [], first
    for rows, _, _ in blocks:
        for h in range(half // LANES):
            filled = rows > h * LANES
            found.append((filled, at))
            at = at + filled.astype(jnp.int32)
    return found, at


def take_units(found, sources, parts, unit_b, total_sum):
    firsts = [sum(parts[:k]) for k in range(len(parts))]
    for (filled, at), refs in zip(found, sources):

        @pl.when(filled)
        def _(at=at, refs=refs):
            pieces = [ref[...].astype(jnp.float32) for ref in refs]
            square = sum(jnp.sum(x * x, axis=-1, keepdims=True) for x in pieces)
            inverse = lax.rsqrt(square + 1e-06)
            for x, first, part in zip(pieces, firsts, parts):
                cols = slice(first, first + part)
                total_sum[:, cols] += jnp.sum(x.reshape(LANES // 8, 8, part), axis=0)
                unit_b[pl.ds(pl.multiple_of(at * LANES, LANES), LANES), cols] = (
                    x * inverse
                ).astype(jnp.bfloat16)


def add_pairs(pairs_ref, first, end, last, hole, unit_b, similar_ref, row_acc, col_acc):
    key = lax.broadcasted_iota(jnp.int32, (ROWS, ROWS), 1)
    query = lax.broadcasted_iota(jnp.int32, (ROWS, ROWS), 0)
    ahead = key - query
    block_of = lambda i: pl.ds(pl.multiple_of(i * ROWS, ROWS), ROWS)

    def pair_of(s, h):
        t = first + s * UNROLL + h
        return pairs_ref[0, t], pairs_ref[1, t], t

    def multiply(s):
        for h in range(UNROLL):
            i, j, _ = pair_of(s, h)
            similar_ref[s % 2, h] = lax.dot_general(
                unit_b[block_of(i), :],
                unit_b[block_of(j), :],
                ACROSS,
                preferred_element_type=jnp.float32,
            )

    def accumulate(s):
        for h in range(UNROLL):
            i, j, t = pair_of(s, h)
            counted = key < jnp.where(t < end, last - j * ROWS, 0)
            counted &= ahead != (i - j) * ROWS
            if hole is not None:
                counted &= (query < hole[0] - i * ROWS) | (query >= hole[1] - i * ROWS)
            terms = jnp.where(counted, jnp.exp(SHARPNESS * similar_ref[s % 2, h]), 0.0)
            row_acc[block_of(i), :] += sum(
                terms[:, k * LANES : (k + 1) * LANES] for k in range(ROWS // LANES)
            )
            sums = jnp.sum(terms.reshape(ROWS // 8, 8, ROWS), axis=0)
            col_acc[:, block_of(j)] += jnp.where(i == j, 0.0, sums)

    steps = (end - first + UNROLL - 1) // UNROLL
    multiply(0)

    def step(s, carry):
        multiply(s)
        accumulate(s - 1)
        return carry

    lax.fori_loop(1, steps, step, 0)
    accumulate(steps - 1)


def start_body(parts, half, info_ref, pairs_ref, *refs):
    per_chunk = 5
    chunks = [refs[k * per_chunk : (k + 1) * per_chunk] for k in range(len(parts))]
    unit_b, row_acc, col_acc, total_sum, similar_ref = refs[len(parts) * per_chunk :]
    blocks = read_plan(info_ref, half)[:6]
    found, units = spots(blocks, half, jnp.int32(0))
    sources = []
    for which, at in [(0, 0), (2, 0), (3, 0), (4, 0), (1, half), (2, half)]:
        for h in range(half // LANES):
            rows = pl.ds(at + h * LANES, LANES)
            sources.append([chunk[which].at[rows] for chunk in chunks])
    total_sum[...] = jnp.zeros_like(total_sum)
    row_acc[...] = jnp.zeros_like(row_acc)
    col_acc[...] = jnp.zeros_like(col_acc)
    take_units(found, sources, parts, unit_b, total_sum)

    @pl.when(units % 2 == 1)
    def _():
        unit_b[pl.ds(pl.multiple_of(units * LANES, LANES), LANES), :] = jnp.zeros(
            (LANES, sum(parts)), jnp.bfloat16
        )

    count = (units + 1) // 2
    end = count * (count + 1) // 2
    add_pairs(
        pairs_ref, 0, end, units * LANES, None, unit_b, similar_ref, row_acc, col_acc
    )


def score_body(parts, half, info_ref, pairs_ref, *refs):
    per_chunk = 2
    chunks = [refs[k * per_chunk : (k + 1) * per_chunk] for k in range(len(parts))]
    refs = refs[len(parts) * per_chunk + 4 :]
    out_ref, unit_b, row_acc, col_acc, total_sum, similar_ref, score_ref = refs
    width = sum(parts)
    per_half = half // LANES
    blocks = read_plan(info_ref, half)
    found, early = spots(blocks[:6], half, jnp.int32(0))
    early_blocks = (early + 1) // 2
    late_found, units = spots(blocks[6:], half, early_blocks * 2)
    count_blocks = units // 2
    first = early_blocks * (early_blocks + 1) // 2
    end = count_blocks * (count_blocks + 1) // 2

    @pl.when(count_blocks > early_blocks)
    def _():
        sources = []
        for which in range(2):
            for h in range(per_half):
                rows = pl.ds(h * LANES, LANES)
                sources.append([chunk[which].at[rows] for chunk in chunks])
        take_units(late_found, sources, parts, unit_b, total_sum)
        hole = (early * LANES, early_blocks * ROWS)
        add_pairs(
            pairs_ref, first, end, units * LANES, hole, unit_b, similar_ref, row_acc, col_acc
        )

    filled_units = early + units - early_blocks * 2
    count = (filled_units * LANES).astype(jnp.float32)
    centroid = jnp.sum(total_sum[...], axis=0, keepdims=True) / count
    direction = centroid * lax.rsqrt(
        jnp.sum(centroid * centroid, axis=-1, keepdims=True) + 1e-06
    )
    high = direction.astype(jnp.bfloat16)
    low = (direction - high.astype(jnp.float32)).astype(jnp.bfloat16)
    row = lax.broadcasted_iota(jnp.int32, (8, width), 0)
    split = jnp.where(
        row == 0,
        high.astype(jnp.float32),
        jnp.where(row == 1, low.astype(jnp.float32), 0.0),
    ).astype(jnp.bfloat16)
    ones = jnp.ones((8, LANES), jnp.float32)
    for b in range(unit_b.shape[0] // ROWS):
        at = slice(b * ROWS, (b + 1) * ROWS)

        @pl.when(b < count_blocks)
        def _(at=at):
            along = lax.dot_general(
                split, unit_b[at, :], ACROSS, preferred_element_type=jnp.float32
            )
            toward = jnp.sum(along, axis=0, keepdims=True)
            rows = lax.dot_general(
                ones,
                row_acc[at, :],
                ACROSS,
                precision=lax.Precision.HIGHEST,
                preferred_element_type=jnp.float32,
            )
            total = rows[:1] + jnp.sum(col_acc[:, at], axis=0, keepdims=True)
            score_ref[:, at] = jnp.log(total) / SHARPNESS - toward

    for s in range(4):
        out_ref[s, : 2 * per_half, :] = jnp.zeros((2 * per_half, LANES), jnp.float32)
        for k in range(width // LANES):
            at = 2 * per_half + k
            out_ref[s, at : at + 1, :] = centroid[:, k * LANES : (k + 1) * LANES]
    for u, (filled, at) in enumerate(found + late_found):
        _, sender, place = blocks[u // per_half]

        @pl.when(filled)
        def _(at=at, to=sender, place=place + u % per_half):
            out_ref[to, place : place + 1, :] = score_ref[
                :, pl.ds(pl.multiple_of(at * LANES, LANES), LANES)
            ]


def start_cluster(info, chunks):
    half = chunks[0][0].shape[0]
    parts = [chunk[0].shape[1] for chunk in chunks]
    width = sum(parts)
    capacity = 8 * half
    flat = [a for chunk in chunks for a in chunk]
    return pl.pallas_call(
        functools.partial(start_body, parts, half),
        in_specs=[smem, smem] + [vmem] * len(flat),
        out_specs=(vmem,) * 4,
        out_shape=(
            jax.ShapeDtypeStruct((capacity, width), jnp.bfloat16),
            jax.ShapeDtypeStruct((capacity, LANES), jnp.float32),
            jax.ShapeDtypeStruct((8, capacity), jnp.float32),
            jax.ShapeDtypeStruct((8, width), jnp.float32),
        ),
        scratch_shapes=[pltpu.VMEM((2, UNROLL, ROWS, ROWS), jnp.float32)],
        cost_estimate=pl.CostEstimate(
            flops=capacity * capacity * width,
            bytes_accessed=2 * capacity * width,
            transcendentals=capacity * capacity // 2,
        ),
        compiler_params=pltpu.CompilerParams(vmem_limit_bytes=SMALL),
        name="start_cluster",
    )(info, jnp.asarray(pair_table(capacity // ROWS)), *flat)


def score_cluster(info, chunks, begun):
    half = chunks[0][0].shape[0]
    parts = [chunk[0].shape[1] for chunk in chunks]
    width = sum(parts)
    capacity = 8 * half
    flat = [a for chunk in chunks for a in chunk]
    lines = 2 * half // LANES + width // LANES
    at = 2 + len(flat)
    out = pl.pallas_call(
        functools.partial(score_body, parts, half),
        in_specs=[smem, smem] + [vmem] * (len(flat) + 4),
        out_specs=(vmem,) * 5,
        out_shape=(jax.ShapeDtypeStruct((4, lines, LANES), jnp.float32),)
        + tuple(jax.ShapeDtypeStruct(a.shape, a.dtype) for a in begun),
        input_output_aliases={at + n: 1 + n for n in range(4)},
        scratch_shapes=[
            pltpu.VMEM((2, UNROLL, ROWS, ROWS), jnp.float32),
            pltpu.VMEM((1, capacity), jnp.float32),
        ],
        cost_estimate=pl.CostEstimate(
            flops=capacity * capacity * width // 4,
            bytes_accessed=2 * capacity * width,
            transcendentals=capacity * capacity // 8,
        ),
        compiler_params=pltpu.CompilerParams(vmem_limit_bytes=SMALL),
        name="score_cluster",
    )(info, jnp.asarray(pair_table(capacity // ROWS)), *flat, *begun)
    return out[0]


def finish_body(info_ref, back_ref, centroid_ref, score_ref):
    per = score_ref.shape[1] // LANES
    for c in range(KC):
        home = info_ref[KC * 4 + HOME + c]
        for k in range(back_ref.shape[1]):
            to, at = (score_ref, k) if k < per else (centroid_ref, k - per)
            to[c : c + 1, at * LANES : (at + 1) * LANES] = back_ref[home, k : k + 1, :]


def finish(info, back, sub, width):
    return pl.pallas_call(
        finish_body,
        in_specs=[smem, vmem],
        out_specs=(vmem, vmem),
        out_shape=(
            jax.ShapeDtypeStruct((KC, width), jnp.float32),
            jax.ShapeDtypeStruct((KC, sub), jnp.float32),
        ),
        name="finish",
    )(info, back)


def swap(x, by):
    return lax.ppermute(x, "own", [(z, z ^ by) for z in range(4)])


def step_move(carried):
    return lax.ppermute(carried, "own", [(1, 2), (2, 1)])


def extra_move(overflow):
    owners = lax.axis_size("rows")
    crossing = [(r * 4 + 2 - r % 2, r * 4 + 1 + r % 2) for r in range(owners)]
    return lax.ppermute(overflow, ("rows", "own"), crossing)


def on_device(emb, send_rows, dest_offset):
    owners = lax.axis_size("rows")
    local, width = emb.shape
    slots = send_rows.shape[2]
    sub = local // 2
    half = sub // 2
    parts = [width // 8 * n for n in EIGHTHS]
    ids = send_rows[0].reshape(-1, ROWS)
    here = lax.axis_index("own")
    owner = lax.axis_index("rows")
    every = lax.all_to_all(
        jnp.repeat(dest_offset[0], 4, axis=0), ("rows", "own"), split_axis=0, concat_axis=0, tiled=True
    )
    every = every.reshape(owners, 4, slots)
    places = lax.dynamic_index_in_dim(every, here, 1, keepdims=False)
    places = places.reshape(1, owners * slots)
    cluster = jnp.arange(KC, dtype=jnp.int32)
    counts = jnp.sum((every[..., None] // sub == cluster).astype(jnp.int32), axis=(0, 2))
    place_value = jnp.asarray([64, 16, 4, 1], jnp.int32)
    index = jnp.sum(jnp.argmax(counts, axis=1).astype(jnp.int32) * place_value)
    index = ((owner % 2) * 256 + index) * 4 + here
    row = lax.dynamic_index_in_dim(jnp.asarray(PLANS), index, 0, keepdims=False)
    info = jnp.concatenate([counts.reshape(-1), row])

    tie = lax.optimization_barrier
    outgoing, moved, carried, steps = [], [], [], []

    def gather(k, ids):
        rows = gather_rows(ids, emb, sum(parts[:k]), parts[k])
        outgoing.append(rows.reshape(owners, slots, parts[k]))

    gather(0, ids)
    ids, info = tie((ids, info))
    gather(1, ids)
    extras = []
    for k, part in enumerate(parts):
        incoming = lax.all_to_all(outgoing[k], "rows", split_axis=0, concat_axis=0, tiled=True)
        incoming = incoming.reshape(owners * slots, part)
        if k:
            incoming, carried[-1] = tie((incoming, carried[-1]))
        two, three = place_rows(info, places, incoming, half, ((2,), (3,)))
        incoming, two = tie((incoming, two))
        kept, pair = place_rows(info, places, incoming, half, ((0,), (1, 4)))
        if k:
            steps.append(step_move(carried[-1]))
            two, three, pair, steps[-1], *last = tie(
                (two, three, pair, steps[-1]) + moved[-1]
            )
            moved[-1] = tuple(last)
        from_two, from_three, from_pair = swap(two, 2), swap(three, 3), swap(pair, 1)
        moved.append((kept, pair, from_pair, from_two, from_three))
        carried.append(
            jnp.where(info[KC * 4 + FORWARD] == 1, from_pair[half:], pair[half:])
        )
    steps.append(step_move(carried[-1]))
    first = moved[-1][2]
    extras = [extra_move(tie((m[1][half:], first))[0]) for m in moved]
    begun = start_cluster(info, moved)
    result = score_cluster(info, list(zip(steps, extras)), begun)
    back = lax.all_to_all(result, "own", split_axis=0, concat_axis=0, tiled=True)
    return finish(info, back, sub, width)


def solution(mesh):
    return jax.shard_map(
        on_device,
        mesh=mesh,
        in_specs=(
            P(("rows", "own"), None),
            P(("rows", "own"), None, None),
            P(("rows", "own"), None, None),
        ),
        out_specs=(P("rows", None), P("rows", "own")),
        check_vma=False,
    )
```

```python
import functools
import itertools

import jax
import jax.numpy as jnp
import numpy as np
from jax import lax
from jax.experimental import pallas as pl
from jax.experimental.pallas import tpu as pltpu
from jax.sharding import PartitionSpec as P

KC = 4
EIGHTHS = (4, 4)
CHUNKS = len(EIGHTHS)
SHARPNESS = 20.0
LANES = 128
ROWS = 256
BIG = 56 << 20
SMALL = 16 << 20
UNROLL = 4

vmem = pl.BlockSpec(memory_space=pltpu.VMEM)
smem = pl.BlockSpec(memory_space=pltpu.SMEM)

HOME, MINE, FORWARD, OWN, PAIR, STEP, EXTRA, STEP_FROM, HERE = 0, 4, 5, 6, 7, 8, 9, 10, 11
PLAN_WIDTH = 16

ACROSS = (((1,), (1,)), ((), ()))


def routes(biggest, home, parity):
    step, extra, kinds = {}, {}, []
    for g in range(4):
        to = home[biggest[g]]
        if to == g:
            kinds.append(OWN)
        elif to == g ^ 1:
            kinds.append(PAIR)
        elif to in (1, 2):
            by = 3 - to
            if by not in step:
                step[by] = g
                kinds.append(STEP)
            else:
                if by != 2 - parity:
                    return None
                pair = {step[by], g}
                if pair != {by, by ^ 1}:
                    return None
                step[by] = by ^ 1
                extra[by] = by
                kinds.append(EXTRA)
        else:
            return None
    return step, extra


def build_plans():
    rows = np.zeros((2, 4, 4, 4, 4, 4, PLAN_WIDTH), np.int32)
    for parity in range(2):
        for biggest in itertools.product(range(4), repeat=4):
            best = None
            for home in itertools.permutations(range(4)):
                found = routes(biggest, home, parity)
                if found is None:
                    continue
                cost = (len(found[1]), len(found[0]))
                if best is None or cost < best[0]:
                    best = (cost, home, found)
            _, home, (step, extra) = best
            for z in range(4):
                row = rows[(parity,) + biggest][z]
                row[HOME : HOME + 4] = home
                row[MINE] = home.index(z)
                row[FORWARD] = int(z in step and step[z] != z)
                row[OWN] = int(home[biggest[z]] == z)
                row[PAIR] = int(home[biggest[z ^ 1]] == z)
                by = 3 - z
                row[STEP] = int(z in (1, 2) and by in step)
                row[STEP_FROM] = step.get(by, 0) if z in (1, 2) else 0
                row[EXTRA] = int(z in (1, 2) and by in extra)
                row[HERE] = z
    return rows.reshape(-1, PLAN_WIDTH)


PLANS = build_plans()


def pair_table(blocks):
    pairs = [(i, j) for j in range(blocks) for i in range(j + 1)]
    pairs += [(0, 0)] * UNROLL
    return np.asarray(pairs, np.int32).T.copy()


def gather_body(first, ids_ref, emb_ref, out_ref, held, rows_ref, sem, sems):
    groups, per = ids_ref.shape
    local, part = held.shape
    fetch = pltpu.make_async_copy(emb_ref.at[:, first : first + part], held, sem)
    fetch.start()
    columns = jnp.transpose(ids_ref[...])
    lane = lax.broadcasted_iota(jnp.int32, (per, local), 1)
    fetch.wait()
    sends = []
    for o in range(groups):
        at = slice(o * per, (o + 1) * per)
        pick = jnp.where(columns[:, o : o + 1] == lane, 1.0, 0.0).astype(jnp.bfloat16)
        rows = jnp.dot(pick, held[...], preferred_element_type=jnp.float32)
        rows_ref[at, :] = rows.astype(jnp.bfloat16)
        sends.append(pltpu.make_async_copy(rows_ref.at[at], out_ref.at[at], sems.at[o]))
        sends[-1].start()
    for send in sends:
        send.wait()


def gather_rows(ids, emb, first, part):
    slots = ids.size
    local = emb.shape[0]
    groups = ids.shape[0]
    return pl.pallas_call(
        functools.partial(gather_body, first),
        in_specs=[vmem, pl.BlockSpec(memory_space=pl.ANY)],
        out_specs=pl.BlockSpec(memory_space=pltpu.HBM),
        out_shape=jax.ShapeDtypeStruct((slots, part), emb.dtype),
        scratch_shapes=[
            pltpu.VMEM((local, part), emb.dtype),
            pltpu.VMEM((slots, part), emb.dtype),
            pltpu.SemaphoreType.DMA,
            pltpu.SemaphoreType.DMA((groups,)),
        ],
        cost_estimate=pl.CostEstimate(
            flops=2 * slots * local * part,
            bytes_accessed=2 * part * (slots + local),
            transcendentals=0,
        ),
        compiler_params=pltpu.CompilerParams(vmem_limit_bytes=BIG),
        name="gather_rows",
    )(ids, emb)


def place_body(blocks, half, info_ref, places_ref, rows_ref, *out_refs):
    arrivals = rows_ref.shape[0]
    here = info_ref[KC * 4 + HERE]
    places = places_ref[...]
    cluster = places // (2 * half)
    inner = places % (2 * half)
    toward = jnp.full_like(places, 8)
    for c in range(KC):
        toward = jnp.where(cluster == c, info_ref[KC * 4 + HOME + c] ^ here, toward)
    target = jnp.where(inner < half, toward * half + inner, 4 * half + inner - half)
    target = jnp.where(cluster < KC, target, -1)
    for ref, inside in zip(out_refs, blocks):
        for n, b in enumerate(inside):
            slot = b * half + lax.broadcasted_iota(jnp.int32, (half, arrivals), 0)
            pick = jnp.where(slot == target, 1.0, 0.0).astype(jnp.bfloat16)
            rows = jnp.dot(pick, rows_ref[...], preferred_element_type=jnp.float32)
            ref[n * half : (n + 1) * half, :] = rows.astype(jnp.bfloat16)


def place_rows(info, places, rows, half, blocks):
    arrivals, part = rows.shape
    sizes = [half * len(inside) for inside in blocks]
    return pl.pallas_call(
        functools.partial(place_body, blocks, half),
        in_specs=[smem, vmem, vmem],
        out_specs=(vmem,) * len(sizes),
        out_shape=tuple(jax.ShapeDtypeStruct((n, part), rows.dtype) for n in sizes),
        cost_estimate=pl.CostEstimate(
            flops=2 * arrivals * sum(sizes) * part,
            bytes_accessed=2 * part * (arrivals + sum(sizes)),
            transcendentals=0,
        ),
        compiler_params=pltpu.CompilerParams(vmem_limit_bytes=SMALL),
        name="place_rows",
    )(info, places, rows)


def read_plan(info_ref, half):
    base = KC * 4
    here = info_ref[base + HERE]
    mine = info_ref[base + MINE]
    blocks = []
    for x in range(4):
        rows = jnp.minimum(info_ref[(here ^ x) * KC + mine], half)
        blocks.append((rows, here ^ x, 0))
    over = [
        (OWN, here),
        (PAIR, here ^ 1),
        (STEP, info_ref[base + STEP_FROM]),
        (EXTRA, 3 - here),
    ]
    for valid, sender in over:
        blocks.append((info_ref[base + valid] * half, sender, half // LANES))
    return blocks


def spots(blocks, half, first):
    found, at = [], first
    for rows, _, _ in blocks:
        for h in range(half // LANES):
            filled = rows > h * LANES
            found.append((filled, at))
            at = at + filled.astype(jnp.int32)
    return found, at


def take_units(found, sources, parts, unit_b, total_sum):
    firsts = [sum(parts[:k]) for k in range(len(parts))]
    for (filled, at), refs in zip(found, sources):

        @pl.when(filled)
        def _(at=at, refs=refs):
            pieces = [ref[...].astype(jnp.float32) for ref in refs]
            square = sum(jnp.sum(x * x, axis=-1, keepdims=True) for x in pieces)
            inverse = lax.rsqrt(square + 1e-06)
            for x, first, part in zip(pieces, firsts, parts):
                cols = slice(first, first + part)
                total_sum[:, cols] += jnp.sum(x.reshape(LANES // 8, 8, part), axis=0)
                unit_b[pl.ds(pl.multiple_of(at * LANES, LANES), LANES), cols] = (
                    x * inverse
                ).astype(jnp.bfloat16)


def add_pairs(pairs_ref, first, end, last, hole, unit_b, similar_ref, row_acc, col_acc):
    key = lax.broadcasted_iota(jnp.int32, (ROWS, ROWS), 1)
    query = lax.broadcasted_iota(jnp.int32, (ROWS, ROWS), 0)
    ahead = key - query
    block_of = lambda i: pl.ds(pl.multiple_of(i * ROWS, ROWS), ROWS)

    def pair_of(s, h):
        t = first + s * UNROLL + h
        return pairs_ref[0, t], pairs_ref[1, t], t

    def multiply(s):
        for h in range(UNROLL):
            i, j, _ = pair_of(s, h)
            similar_ref[s % 2, h] = lax.dot_general(
                unit_b[block_of(i), :],
                unit_b[block_of(j), :],
                ACROSS,
                preferred_element_type=jnp.float32,
            )

    def accumulate(s):
        for h in range(UNROLL):
            i, j, t = pair_of(s, h)
            counted = key < jnp.where(t < end, last - j * ROWS, 0)
            counted &= ahead != (i - j) * ROWS
            if hole is not None:
                counted &= (query < hole[0] - i * ROWS) | (query >= hole[1] - i * ROWS)
            terms = jnp.where(counted, jnp.exp(SHARPNESS * similar_ref[s % 2, h]), 0.0)
            row_acc[block_of(i), :] += sum(
                terms[:, k * LANES : (k + 1) * LANES] for k in range(ROWS // LANES)
            )
            sums = jnp.sum(terms.reshape(ROWS // 8, 8, ROWS), axis=0)
            col_acc[:, block_of(j)] += jnp.where(i == j, 0.0, sums)

    steps = (end - first + UNROLL - 1) // UNROLL
    multiply(0)

    def step(s, carry):
        multiply(s)
        accumulate(s - 1)
        return carry

    lax.fori_loop(1, steps, step, 0)
    accumulate(steps - 1)


def start_body(parts, half, info_ref, pairs_ref, *refs):
    per_chunk = 5
    chunks = [refs[k * per_chunk : (k + 1) * per_chunk] for k in range(len(parts))]
    unit_b, row_acc, col_acc, total_sum, similar_ref = refs[len(parts) * per_chunk :]
    blocks = read_plan(info_ref, half)[:6]
    found, units = spots(blocks, half, jnp.int32(0))
    sources = []
    for which, at in [(0, 0), (2, 0), (3, 0), (4, 0), (1, half), (2, half)]:
        for h in range(half // LANES):
            rows = pl.ds(at + h * LANES, LANES)
            sources.append([chunk[which].at[rows] for chunk in chunks])
    total_sum[...] = jnp.zeros_like(total_sum)
    row_acc[...] = jnp.zeros_like(row_acc)
    col_acc[...] = jnp.zeros_like(col_acc)
    take_units(found, sources, parts, unit_b, total_sum)

    @pl.when(units % 2 == 1)
    def _():
        unit_b[pl.ds(pl.multiple_of(units * LANES, LANES), LANES), :] = jnp.zeros(
            (LANES, sum(parts)), jnp.bfloat16
        )

    count = (units + 1) // 2
    end = count * (count + 1) // 2
    add_pairs(
        pairs_ref, 0, end, units * LANES, None, unit_b, similar_ref, row_acc, col_acc
    )


def score_body(parts, half, info_ref, pairs_ref, *refs):
    per_chunk = 2
    chunks = [refs[k * per_chunk : (k + 1) * per_chunk] for k in range(len(parts))]
    refs = refs[len(parts) * per_chunk + 4 :]
    out_ref, unit_b, row_acc, col_acc, total_sum, similar_ref, score_ref = refs
    width = sum(parts)
    per_half = half // LANES
    blocks = read_plan(info_ref, half)
    found, early = spots(blocks[:6], half, jnp.int32(0))
    early_blocks = (early + 1) // 2
    late_found, units = spots(blocks[6:], half, early_blocks * 2)
    count_blocks = units // 2
    first = early_blocks * (early_blocks + 1) // 2
    end = count_blocks * (count_blocks + 1) // 2

    @pl.when(count_blocks > early_blocks)
    def _():
        sources = []
        for which in range(2):
            for h in range(per_half):
                rows = pl.ds(h * LANES, LANES)
                sources.append([chunk[which].at[rows] for chunk in chunks])
        take_units(late_found, sources, parts, unit_b, total_sum)
        hole = (early * LANES, early_blocks * ROWS)
        add_pairs(
            pairs_ref, first, end, units * LANES, hole, unit_b, similar_ref, row_acc, col_acc
        )

    filled_units = early + units - early_blocks * 2
    count = (filled_units * LANES).astype(jnp.float32)
    centroid = jnp.sum(total_sum[...], axis=0, keepdims=True) / count
    direction = centroid * lax.rsqrt(
        jnp.sum(centroid * centroid, axis=-1, keepdims=True) + 1e-06
    )
    high = direction.astype(jnp.bfloat16)
    low = (direction - high.astype(jnp.float32)).astype(jnp.bfloat16)
    row = lax.broadcasted_iota(jnp.int32, (8, width), 0)
    split = jnp.where(
        row == 0,
        high.astype(jnp.float32),
        jnp.where(row == 1, low.astype(jnp.float32), 0.0),
    ).astype(jnp.bfloat16)
    ones = jnp.ones((8, LANES), jnp.float32)
    along = lax.dot_general(
        split, unit_b[...], ACROSS, preferred_element_type=jnp.float32
    )
    toward = jnp.sum(along, axis=0, keepdims=True)
    rows = lax.dot_general(
        ones,
        row_acc[...],
        ACROSS,
        precision=lax.Precision.HIGHEST,
        preferred_element_type=jnp.float32,
    )
    total = rows[:1] + jnp.sum(col_acc[...], axis=0, keepdims=True)
    score_ref[...] = jnp.log(total) / SHARPNESS - toward

    for s in range(4):
        out_ref[s, : 2 * per_half, :] = jnp.zeros((2 * per_half, LANES), jnp.float32)
        for k in range(width // LANES):
            at = 2 * per_half + k
            out_ref[s, at : at + 1, :] = centroid[:, k * LANES : (k + 1) * LANES]
    for u, (filled, at) in enumerate(found + late_found):
        _, sender, place = blocks[u // per_half]

        @pl.when(filled)
        def _(at=at, to=sender, place=place + u % per_half):
            out_ref[to, place : place + 1, :] = score_ref[
                :, pl.ds(pl.multiple_of(at * LANES, LANES), LANES)
            ]


def start_cluster(info, chunks):
    half = chunks[0][0].shape[0]
    parts = [chunk[0].shape[1] for chunk in chunks]
    width = sum(parts)
    capacity = 8 * half
    flat = [a for chunk in chunks for a in chunk]
    return pl.pallas_call(
        functools.partial(start_body, parts, half),
        in_specs=[smem, smem] + [vmem] * len(flat),
        out_specs=(vmem,) * 4,
        out_shape=(
            jax.ShapeDtypeStruct((capacity, width), jnp.bfloat16),
            jax.ShapeDtypeStruct((capacity, LANES), jnp.float32),
            jax.ShapeDtypeStruct((8, capacity), jnp.float32),
            jax.ShapeDtypeStruct((8, width), jnp.float32),
        ),
        scratch_shapes=[pltpu.VMEM((2, UNROLL, ROWS, ROWS), jnp.float32)],
        cost_estimate=pl.CostEstimate(
            flops=capacity * capacity * width,
            bytes_accessed=2 * capacity * width,
            transcendentals=capacity * capacity // 2,
        ),
        compiler_params=pltpu.CompilerParams(vmem_limit_bytes=SMALL),
        name="start_cluster",
    )(info, jnp.asarray(pair_table(capacity // ROWS)), *flat)


def score_cluster(info, chunks, begun):
    half = chunks[0][0].shape[0]
    parts = [chunk[0].shape[1] for chunk in chunks]
    width = sum(parts)
    capacity = 8 * half
    flat = [a for chunk in chunks for a in chunk]
    lines = 2 * half // LANES + width // LANES
    at = 2 + len(flat)
    out = pl.pallas_call(
        functools.partial(score_body, parts, half),
        in_specs=[smem, smem] + [vmem] * (len(flat) + 4),
        out_specs=(vmem,) * 5,
        out_shape=(jax.ShapeDtypeStruct((4, lines, LANES), jnp.float32),)
        + tuple(jax.ShapeDtypeStruct(a.shape, a.dtype) for a in begun),
        input_output_aliases={at + n: 1 + n for n in range(4)},
        scratch_shapes=[
            pltpu.VMEM((2, UNROLL, ROWS, ROWS), jnp.float32),
            pltpu.VMEM((1, capacity), jnp.float32),
        ],
        cost_estimate=pl.CostEstimate(
            flops=capacity * capacity * width // 4,
            bytes_accessed=2 * capacity * width,
            transcendentals=capacity * capacity // 8,
        ),
        compiler_params=pltpu.CompilerParams(vmem_limit_bytes=SMALL),
        name="score_cluster",
    )(info, jnp.asarray(pair_table(capacity // ROWS)), *flat, *begun)
    return out[0]


def finish_body(info_ref, back_ref, centroid_ref, score_ref):
    per = score_ref.shape[1] // LANES
    for c in range(KC):
        home = info_ref[KC * 4 + HOME + c]
        for k in range(back_ref.shape[1]):
            to, at = (score_ref, k) if k < per else (centroid_ref, k - per)
            to[c : c + 1, at * LANES : (at + 1) * LANES] = back_ref[home, k : k + 1, :]


def finish(info, back, sub, width):
    return pl.pallas_call(
        finish_body,
        in_specs=[smem, vmem],
        out_specs=(vmem, vmem),
        out_shape=(
            jax.ShapeDtypeStruct((KC, width), jnp.float32),
            jax.ShapeDtypeStruct((KC, sub), jnp.float32),
        ),
        name="finish",
    )(info, back)


def swap(x, by):
    return lax.ppermute(x, "own", [(z, z ^ by) for z in range(4)])


def step_move(carried):
    return lax.ppermute(carried, "own", [(1, 2), (2, 1)])


def extra_move(overflow):
    owners = lax.axis_size("rows")
    crossing = [(r * 4 + 2 - r % 2, r * 4 + 1 + r % 2) for r in range(owners)]
    return lax.ppermute(overflow, ("rows", "own"), crossing)


def on_device(emb, send_rows, dest_offset):
    owners = lax.axis_size("rows")
    local, width = emb.shape
    slots = send_rows.shape[2]
    sub = local // 2
    half = sub // 2
    parts = [width // 8 * n for n in EIGHTHS]
    ids = send_rows[0].reshape(-1, ROWS)
    here = lax.axis_index("own")
    owner = lax.axis_index("rows")
    every = lax.all_to_all(
        jnp.repeat(dest_offset[0], 4, axis=0), ("rows", "own"), split_axis=0, concat_axis=0, tiled=True
    )
    every = every.reshape(owners, 4, slots)
    places = lax.dynamic_index_in_dim(every, here, 1, keepdims=False)
    places = places.reshape(1, owners * slots)
    cluster = jnp.arange(KC, dtype=jnp.int32)
    counts = jnp.sum((every[..., None] // sub == cluster).astype(jnp.int32), axis=(0, 2))
    place_value = jnp.asarray([64, 16, 4, 1], jnp.int32)
    index = jnp.sum(jnp.argmax(counts, axis=1).astype(jnp.int32) * place_value)
    index = ((owner % 2) * 256 + index) * 4 + here
    row = lax.dynamic_index_in_dim(jnp.asarray(PLANS), index, 0, keepdims=False)
    info = jnp.concatenate([counts.reshape(-1), row])

    tie = lax.optimization_barrier
    outgoing, moved, carried, steps = [], [], [], []

    def gather(k, ids):
        rows = gather_rows(ids, emb, sum(parts[:k]), parts[k])
        outgoing.append(rows.reshape(owners, slots, parts[k]))

    gather(0, ids)
    ids, info = tie((ids, info))
    gather(1, ids)
    extras = []
    for k, part in enumerate(parts):
        incoming = lax.all_to_all(outgoing[k], "rows", split_axis=0, concat_axis=0, tiled=True)
        incoming = incoming.reshape(owners * slots, part)
        if k:
            incoming, carried[-1] = tie((incoming, carried[-1]))
        two, three = place_rows(info, places, incoming, half, ((2,), (3,)))
        incoming, two = tie((incoming, two))
        kept, pair = place_rows(info, places, incoming, half, ((0,), (1, 4)))
        if k:
            steps.append(step_move(carried[-1]))
            two, three, pair, steps[-1], *last = tie(
                (two, three, pair, steps[-1]) + moved[-1]
            )
            moved[-1] = tuple(last)
        from_two, from_three, from_pair = swap(two, 2), swap(three, 3), swap(pair, 1)
        moved.append((kept, pair, from_pair, from_two, from_three))
        carried.append(
            jnp.where(info[KC * 4 + FORWARD] == 1, from_pair[half:], pair[half:])
        )
    steps.append(step_move(carried[-1]))
    first = carried[-1]
    extras = [extra_move(tie((m[1][half:], first))[0]) for m in moved]
    begun = start_cluster(info, moved)
    result = score_cluster(info, list(zip(steps, extras)), begun)
    back = lax.all_to_all(result, "own", split_axis=0, concat_axis=0, tiled=True)
    return finish(info, back, sub, width)


def solution(mesh):
    return jax.shard_map(
        on_device,
        mesh=mesh,
        in_specs=(
            P(("rows", "own"), None),
            P(("rows", "own"), None, None),
            P(("rows", "own"), None, None),
        ),
        out_specs=(P("rows", None), P("rows", "own")),
        check_vma=False,
    )
```

```python
import functools
import itertools

import jax
import jax.numpy as jnp
import numpy as np
from jax import lax
from jax.experimental import pallas as pl
from jax.experimental.pallas import tpu as pltpu
from jax.sharding import PartitionSpec as P

KC = 4
EIGHTHS = (4, 4)
CHUNKS = len(EIGHTHS)
SHARPNESS = 20.0
LANES = 128
ROWS = 256
BIG = 56 << 20
SMALL = 16 << 20
UNROLL = 4

vmem = pl.BlockSpec(memory_space=pltpu.VMEM)
smem = pl.BlockSpec(memory_space=pltpu.SMEM)

HOME, MINE, FORWARD, OWN, PAIR, STEP, EXTRA, STEP_FROM, HERE = 0, 4, 5, 6, 7, 8, 9, 10, 11
PLAN_WIDTH = 16

ACROSS = (((1,), (1,)), ((), ()))


def routes(biggest, home, parity):
    step, extra, kinds = {}, {}, []
    for g in range(4):
        to = home[biggest[g]]
        if to == g:
            kinds.append(OWN)
        elif to == g ^ 1:
            kinds.append(PAIR)
        elif to in (1, 2):
            by = 3 - to
            if by not in step:
                step[by] = g
                kinds.append(STEP)
            else:
                if by != 2 - parity:
                    return None
                pair = {step[by], g}
                if pair != {by, by ^ 1}:
                    return None
                step[by] = by ^ 1
                extra[by] = by
                kinds.append(EXTRA)
        else:
            return None
    return step, extra


def build_plans():
    rows = np.zeros((2, 4, 4, 4, 4, 4, PLAN_WIDTH), np.int32)
    for parity in range(2):
        for biggest in itertools.product(range(4), repeat=4):
            best = None
            for home in itertools.permutations(range(4)):
                found = routes(biggest, home, parity)
                if found is None:
                    continue
                cost = (len(found[1]), len(found[0]))
                if best is None or cost < best[0]:
                    best = (cost, home, found)
            _, home, (step, extra) = best
            for z in range(4):
                row = rows[(parity,) + biggest][z]
                row[HOME : HOME + 4] = home
                row[MINE] = home.index(z)
                row[FORWARD] = int(z in step and step[z] != z)
                row[OWN] = int(home[biggest[z]] == z)
                row[PAIR] = int(home[biggest[z ^ 1]] == z)
                by = 3 - z
                row[STEP] = int(z in (1, 2) and by in step)
                row[STEP_FROM] = step.get(by, 0) if z in (1, 2) else 0
                row[EXTRA] = int(z in (1, 2) and by in extra)
                row[HERE] = z
    return rows.reshape(-1, PLAN_WIDTH)


PLANS = build_plans()


def pair_table(blocks):
    pairs = [(i, j) for j in range(blocks) for i in range(j + 1)]
    pairs += [(0, 0)] * UNROLL
    return np.asarray(pairs, np.int32).T.copy()


def gather_body(first, ids_ref, emb_ref, out_ref, held, rows_ref, sem, sems):
    groups, per = ids_ref.shape
    local, part = held.shape
    fetch = pltpu.make_async_copy(emb_ref.at[:, first : first + part], held, sem)
    fetch.start()
    columns = jnp.transpose(ids_ref[...])
    lane = lax.broadcasted_iota(jnp.int32, (per, local), 1)
    fetch.wait()
    sends = []
    for o in range(groups):
        at = slice(o * per, (o + 1) * per)
        pick = jnp.where(columns[:, o : o + 1] == lane, 1.0, 0.0).astype(jnp.bfloat16)
        rows = jnp.dot(pick, held[...], preferred_element_type=jnp.float32)
        rows_ref[at, :] = rows.astype(jnp.bfloat16)
        sends.append(pltpu.make_async_copy(rows_ref.at[at], out_ref.at[at], sems.at[o]))
        sends[-1].start()
    for send in sends:
        send.wait()


def gather_rows(ids, emb, first, part):
    slots = ids.size
    local = emb.shape[0]
    groups = ids.shape[0]
    return pl.pallas_call(
        functools.partial(gather_body, first),
        in_specs=[vmem, pl.BlockSpec(memory_space=pl.ANY)],
        out_specs=pl.BlockSpec(memory_space=pltpu.HBM),
        out_shape=jax.ShapeDtypeStruct((slots, part), emb.dtype),
        scratch_shapes=[
            pltpu.VMEM((local, part), emb.dtype),
            pltpu.VMEM((slots, part), emb.dtype),
            pltpu.SemaphoreType.DMA,
            pltpu.SemaphoreType.DMA((groups,)),
        ],
        cost_estimate=pl.CostEstimate(
            flops=2 * slots * local * part,
            bytes_accessed=2 * part * (slots + local),
            transcendentals=0,
        ),
        compiler_params=pltpu.CompilerParams(vmem_limit_bytes=BIG),
        name="gather_rows",
    )(ids, emb)


def place_body(blocks, half, info_ref, places_ref, rows_ref, *out_refs):
    arrivals = rows_ref.shape[0]
    here = info_ref[KC * 4 + HERE]
    places = places_ref[...]
    cluster = places // (2 * half)
    inner = places % (2 * half)
    toward = jnp.full_like(places, 8)
    for c in range(KC):
        toward = jnp.where(cluster == c, info_ref[KC * 4 + HOME + c] ^ here, toward)
    target = jnp.where(inner < half, toward * half + inner, 4 * half + inner - half)
    target = jnp.where(cluster < KC, target, -1)
    for ref, inside in zip(out_refs, blocks):
        for n, b in enumerate(inside):
            slot = b * half + lax.broadcasted_iota(jnp.int32, (half, arrivals), 0)
            pick = jnp.where(slot == target, 1.0, 0.0).astype(jnp.bfloat16)
            rows = jnp.dot(pick, rows_ref[...], preferred_element_type=jnp.float32)
            ref[n * half : (n + 1) * half, :] = rows.astype(jnp.bfloat16)


def place_rows(info, places, rows, half, blocks):
    arrivals, part = rows.shape
    sizes = [half * len(inside) for inside in blocks]
    return pl.pallas_call(
        functools.partial(place_body, blocks, half),
        in_specs=[smem, vmem, vmem],
        out_specs=(vmem,) * len(sizes),
        out_shape=tuple(jax.ShapeDtypeStruct((n, part), rows.dtype) for n in sizes),
        cost_estimate=pl.CostEstimate(
            flops=2 * arrivals * sum(sizes) * part,
            bytes_accessed=2 * part * (arrivals + sum(sizes)),
            transcendentals=0,
        ),
        compiler_params=pltpu.CompilerParams(vmem_limit_bytes=SMALL),
        name="place_rows",
    )(info, places, rows)


def read_plan(info_ref, half):
    base = KC * 4
    here = info_ref[base + HERE]
    mine = info_ref[base + MINE]
    blocks = []
    for x in range(4):
        rows = jnp.minimum(info_ref[(here ^ x) * KC + mine], half)
        blocks.append((rows, here ^ x, 0))
    over = [
        (OWN, here),
        (PAIR, here ^ 1),
        (STEP, info_ref[base + STEP_FROM]),
        (EXTRA, 3 - here),
    ]
    for valid, sender in over:
        blocks.append((info_ref[base + valid] * half, sender, half // LANES))
    return blocks


def spots(blocks, half, first):
    found, at = [], first
    for rows, _, _ in blocks:
        for h in range(half // LANES):
            filled = rows > h * LANES
            found.append((filled, at))
            at = at + filled.astype(jnp.int32)
    return found, at


def take_units(found, sources, parts, unit_b, total_sum):
    firsts = [sum(parts[:k]) for k in range(len(parts))]
    for (filled, at), refs in zip(found, sources):

        @pl.when(filled)
        def _(at=at, refs=refs):
            pieces = [ref[...].astype(jnp.float32) for ref in refs]
            square = sum(jnp.sum(x * x, axis=-1, keepdims=True) for x in pieces)
            inverse = lax.rsqrt(square + 1e-06)
            for x, first, part in zip(pieces, firsts, parts):
                cols = slice(first, first + part)
                total_sum[:, cols] += jnp.sum(x.reshape(LANES // 8, 8, part), axis=0)
                unit_b[pl.ds(pl.multiple_of(at * LANES, LANES), LANES), cols] = (
                    x * inverse
                ).astype(jnp.bfloat16)


def add_pairs(pairs_ref, first, end, last, hole, unit_b, similar_ref, row_acc, col_acc):
    key = lax.broadcasted_iota(jnp.int32, (ROWS, ROWS), 1)
    query = lax.broadcasted_iota(jnp.int32, (ROWS, ROWS), 0)
    ahead = key - query
    block_of = lambda i: pl.ds(pl.multiple_of(i * ROWS, ROWS), ROWS)

    def pair_of(s, h):
        t = first + s * UNROLL + h
        return pairs_ref[0, t], pairs_ref[1, t], t

    def multiply(s):
        for h in range(UNROLL):
            i, j, _ = pair_of(s, h)
            similar_ref[s % 2, h] = lax.dot_general(
                unit_b[block_of(i), :],
                unit_b[block_of(j), :],
                ACROSS,
                preferred_element_type=jnp.float32,
            )

    def accumulate(s):
        for h in range(UNROLL):
            i, j, t = pair_of(s, h)
            counted = key < jnp.where(t < end, last - j * ROWS, 0)
            counted &= ahead != (i - j) * ROWS
            if hole is not None:
                counted &= (query < hole[0] - i * ROWS) | (query >= hole[1] - i * ROWS)
            terms = jnp.where(counted, jnp.exp(SHARPNESS * similar_ref[s % 2, h]), 0.0)
            row_acc[block_of(i), :] += sum(
                terms[:, k * LANES : (k + 1) * LANES] for k in range(ROWS // LANES)
            )
            sums = jnp.sum(terms.reshape(ROWS // 8, 8, ROWS), axis=0)
            col_acc[:, block_of(j)] += jnp.where(i == j, 0.0, sums)

    steps = (end - first + UNROLL - 1) // UNROLL
    multiply(0)

    def step(s, carry):
        multiply(s)
        accumulate(s - 1)
        return carry

    lax.fori_loop(1, steps, step, 0)
    accumulate(steps - 1)


def start_body(parts, half, info_ref, pairs_ref, *refs):
    per_chunk = 5
    chunks = [refs[k * per_chunk : (k + 1) * per_chunk] for k in range(len(parts))]
    unit_b, row_acc, col_acc, total_sum, similar_ref = refs[len(parts) * per_chunk :]
    blocks = read_plan(info_ref, half)[:6]
    found, units = spots(blocks, half, jnp.int32(0))
    sources = []
    for which, at in [(0, 0), (2, 0), (3, 0), (4, 0), (1, half), (2, half)]:
        for h in range(half // LANES):
            rows = pl.ds(at + h * LANES, LANES)
            sources.append([chunk[which].at[rows] for chunk in chunks])
    total_sum[...] = jnp.zeros_like(total_sum)
    row_acc[...] = jnp.zeros_like(row_acc)
    col_acc[...] = jnp.zeros_like(col_acc)
    take_units(found, sources, parts, unit_b, total_sum)

    @pl.when(units % 2 == 1)
    def _():
        unit_b[pl.ds(pl.multiple_of(units * LANES, LANES), LANES), :] = jnp.zeros(
            (LANES, sum(parts)), jnp.bfloat16
        )

    count = (units + 1) // 2
    end = count * (count + 1) // 2
    add_pairs(
        pairs_ref, 0, end, units * LANES, None, unit_b, similar_ref, row_acc, col_acc
    )


def score_body(parts, half, info_ref, pairs_ref, *refs):
    per_chunk = 2
    chunks = [refs[k * per_chunk : (k + 1) * per_chunk] for k in range(len(parts))]
    refs = refs[len(parts) * per_chunk + 4 :]
    out_ref, unit_b, row_acc, col_acc, total_sum, similar_ref, score_ref = refs
    width = sum(parts)
    per_half = half // LANES
    blocks = read_plan(info_ref, half)
    found, early = spots(blocks[:6], half, jnp.int32(0))
    early_blocks = (early + 1) // 2
    late_found, units = spots(blocks[6:], half, early_blocks * 2)
    count_blocks = units // 2
    first = early_blocks * (early_blocks + 1) // 2
    end = count_blocks * (count_blocks + 1) // 2

    @pl.when(count_blocks > early_blocks)
    def _():
        sources = []
        for which in range(2):
            for h in range(per_half):
                rows = pl.ds(h * LANES, LANES)
                sources.append([chunk[which].at[rows] for chunk in chunks])
        take_units(late_found, sources, parts, unit_b, total_sum)
        hole = (early * LANES, early_blocks * ROWS)
        add_pairs(
            pairs_ref, first, end, units * LANES, hole, unit_b, similar_ref, row_acc, col_acc
        )

    filled_units = early + units - early_blocks * 2
    count = (filled_units * LANES).astype(jnp.float32)
    centroid = jnp.sum(total_sum[...], axis=0, keepdims=True) / count
    direction = centroid * lax.rsqrt(
        jnp.sum(centroid * centroid, axis=-1, keepdims=True) + 1e-06
    )
    high = direction.astype(jnp.bfloat16)
    low = (direction - high.astype(jnp.float32)).astype(jnp.bfloat16)
    row = lax.broadcasted_iota(jnp.int32, (8, width), 0)
    split = jnp.where(
        row == 0,
        high.astype(jnp.float32),
        jnp.where(row == 1, low.astype(jnp.float32), 0.0),
    ).astype(jnp.bfloat16)
    ones = jnp.ones((8, LANES), jnp.bfloat16)
    along = lax.dot_general(
        split, unit_b[...], ACROSS, preferred_element_type=jnp.float32
    )
    toward = jnp.sum(along, axis=0, keepdims=True)
    sums_high = row_acc[...].astype(jnp.bfloat16)
    sums_low = (row_acc[...] - sums_high.astype(jnp.float32)).astype(jnp.bfloat16)
    rows = lax.dot_general(
        ones, sums_high, ACROSS, preferred_element_type=jnp.float32
    ) + lax.dot_general(ones, sums_low, ACROSS, preferred_element_type=jnp.float32)
    total = rows[:1] + jnp.sum(col_acc[...], axis=0, keepdims=True)
    score_ref[...] = jnp.log(total) / SHARPNESS - toward

    for s in range(4):
        out_ref[s, : 2 * per_half, :] = jnp.zeros((2 * per_half, LANES), jnp.float32)
        for k in range(width // LANES):
            at = 2 * per_half + k
            out_ref[s, at : at + 1, :] = centroid[:, k * LANES : (k + 1) * LANES]
    for u, (filled, at) in enumerate(found + late_found):
        _, sender, place = blocks[u // per_half]

        @pl.when(filled)
        def _(at=at, to=sender, place=place + u % per_half):
            out_ref[to, place : place + 1, :] = score_ref[
                :, pl.ds(pl.multiple_of(at * LANES, LANES), LANES)
            ]


def start_cluster(info, chunks):
    half = chunks[0][0].shape[0]
    parts = [chunk[0].shape[1] for chunk in chunks]
    width = sum(parts)
    capacity = 8 * half
    flat = [a for chunk in chunks for a in chunk]
    return pl.pallas_call(
        functools.partial(start_body, parts, half),
        in_specs=[smem, smem] + [vmem] * len(flat),
        out_specs=(vmem,) * 4,
        out_shape=(
            jax.ShapeDtypeStruct((capacity, width), jnp.bfloat16),
            jax.ShapeDtypeStruct((capacity, LANES), jnp.float32),
            jax.ShapeDtypeStruct((8, capacity), jnp.float32),
            jax.ShapeDtypeStruct((8, width), jnp.float32),
        ),
        scratch_shapes=[pltpu.VMEM((2, UNROLL, ROWS, ROWS), jnp.float32)],
        cost_estimate=pl.CostEstimate(
            flops=capacity * capacity * width,
            bytes_accessed=2 * capacity * width,
            transcendentals=capacity * capacity // 2,
        ),
        compiler_params=pltpu.CompilerParams(vmem_limit_bytes=SMALL),
        name="start_cluster",
    )(info, jnp.asarray(pair_table(capacity // ROWS)), *flat)


def score_cluster(info, chunks, begun):
    half = chunks[0][0].shape[0]
    parts = [chunk[0].shape[1] for chunk in chunks]
    width = sum(parts)
    capacity = 8 * half
    flat = [a for chunk in chunks for a in chunk]
    lines = 2 * half // LANES + width // LANES
    at = 2 + len(flat)
    out = pl.pallas_call(
        functools.partial(score_body, parts, half),
        in_specs=[smem, smem] + [vmem] * (len(flat) + 4),
        out_specs=(vmem,) * 5,
        out_shape=(jax.ShapeDtypeStruct((4, lines, LANES), jnp.float32),)
        + tuple(jax.ShapeDtypeStruct(a.shape, a.dtype) for a in begun),
        input_output_aliases={at + n: 1 + n for n in range(4)},
        scratch_shapes=[
            pltpu.VMEM((2, UNROLL, ROWS, ROWS), jnp.float32),
            pltpu.VMEM((1, capacity), jnp.float32),
        ],
        cost_estimate=pl.CostEstimate(
            flops=capacity * capacity * width // 4,
            bytes_accessed=2 * capacity * width,
            transcendentals=capacity * capacity // 8,
        ),
        compiler_params=pltpu.CompilerParams(vmem_limit_bytes=SMALL),
        name="score_cluster",
    )(info, jnp.asarray(pair_table(capacity // ROWS)), *flat, *begun)
    return out[0]


def finish_body(info_ref, back_ref, centroid_ref, score_ref):
    per = score_ref.shape[1] // LANES
    for c in range(KC):
        home = info_ref[KC * 4 + HOME + c]
        for k in range(back_ref.shape[1]):
            to, at = (score_ref, k) if k < per else (centroid_ref, k - per)
            to[c : c + 1, at * LANES : (at + 1) * LANES] = back_ref[home, k : k + 1, :]


def finish(info, back, sub, width):
    return pl.pallas_call(
        finish_body,
        in_specs=[smem, vmem],
        out_specs=(vmem, vmem),
        out_shape=(
            jax.ShapeDtypeStruct((KC, width), jnp.float32),
            jax.ShapeDtypeStruct((KC, sub), jnp.float32),
        ),
        name="finish",
    )(info, back)


def swap(x, by):
    return lax.ppermute(x, "own", [(z, z ^ by) for z in range(4)])


def step_move(carried):
    return lax.ppermute(carried, "own", [(1, 2), (2, 1)])


def extra_move(overflow):
    owners = lax.axis_size("rows")
    crossing = [(r * 4 + 2 - r % 2, r * 4 + 1 + r % 2) for r in range(owners)]
    return lax.ppermute(overflow, ("rows", "own"), crossing)


def on_device(emb, send_rows, dest_offset):
    owners = lax.axis_size("rows")
    local, width = emb.shape
    slots = send_rows.shape[2]
    sub = local // 2
    half = sub // 2
    parts = [width // 8 * n for n in EIGHTHS]
    ids = send_rows[0].reshape(-1, ROWS)
    here = lax.axis_index("own")
    owner = lax.axis_index("rows")
    every = lax.all_to_all(
        jnp.repeat(dest_offset[0], 4, axis=0), ("rows", "own"), split_axis=0, concat_axis=0, tiled=True
    )
    every = every.reshape(owners, 4, slots)
    places = lax.dynamic_index_in_dim(every, here, 1, keepdims=False)
    places = places.reshape(1, owners * slots)
    cluster = jnp.arange(KC, dtype=jnp.int32)
    counts = jnp.sum((every[..., None] // sub == cluster).astype(jnp.int32), axis=(0, 2))
    place_value = jnp.asarray([64, 16, 4, 1], jnp.int32)
    index = jnp.sum(jnp.argmax(counts, axis=1).astype(jnp.int32) * place_value)
    index = ((owner % 2) * 256 + index) * 4 + here
    row = lax.dynamic_index_in_dim(jnp.asarray(PLANS), index, 0, keepdims=False)
    info = jnp.concatenate([counts.reshape(-1), row])

    tie = lax.optimization_barrier
    outgoing, moved, carried, steps = [], [], [], []

    def gather(k, ids):
        rows = gather_rows(ids, emb, sum(parts[:k]), parts[k])
        outgoing.append(rows.reshape(owners, slots, parts[k]))

    gather(0, ids)
    ids, info = tie((ids, info))
    gather(1, ids)
    extras = []
    for k, part in enumerate(parts):
        incoming = lax.all_to_all(outgoing[k], "rows", split_axis=0, concat_axis=0, tiled=True)
        incoming = incoming.reshape(owners * slots, part)
        if k:
            incoming, carried[-1] = tie((incoming, carried[-1]))
        two, three = place_rows(info, places, incoming, half, ((2,), (3,)))
        incoming, two = tie((incoming, two))
        kept, pair = place_rows(info, places, incoming, half, ((0,), (1, 4)))
        if k:
            steps.append(step_move(carried[-1]))
            two, three, pair, steps[-1], *last = tie(
                (two, three, pair, steps[-1]) + moved[-1]
            )
            moved[-1] = tuple(last)
        from_two, from_three, from_pair = swap(two, 2), swap(three, 3), swap(pair, 1)
        moved.append((kept, pair, from_pair, from_two, from_three))
        carried.append(
            jnp.where(info[KC * 4 + FORWARD] == 1, from_pair[half:], pair[half:])
        )
    steps.append(step_move(carried[-1]))
    first = carried[-1]
    extras = [extra_move(tie((m[1][half:], first))[0]) for m in moved]
    begun = start_cluster(info, moved)
    result = score_cluster(info, list(zip(steps, extras)), begun)
    back = lax.all_to_all(result, "own", split_axis=0, concat_axis=0, tiled=True)
    return finish(info, back, sub, width)


def solution(mesh):
    return jax.shard_map(
        on_device,
        mesh=mesh,
        in_specs=(
            P(("rows", "own"), None),
            P(("rows", "own"), None, None),
            P(("rows", "own"), None, None),
        ),
        out_specs=(P("rows", None), P("rows", "own")),
        check_vma=False,
    )
```
